512 devices in a mesh: chain: 8 (over y), rows: 32 (over x, z), clip: 2 (over core).
Axes of the slice: x: 4, y: 8, z: 8, core: 2. Of those that a mesh axis runs over, the one named last changes fastest.
Arguments:
- video: bfloat16 [2, 16, 64, 48, 384], P('clip', 'chain', 'rows'), may hold values from -6 to 6
- cotangent: bfloat16 [2, 32, 128, 96, 192], P('clip', 'chain', 'rows'), may hold values from -6 to 6
- w_time: bfloat16 [3, 384, 768], replicated, may hold values from -0.1875 to 0.1875
- w_space: bfloat16 [3, 3, 384, 192], replicated, may hold values from -0.109375 to 0.109375
Outputs:
- grad_video: bfloat16 [2, 16, 64, 48, 384], P('clip', 'chain', 'rows')
- grad_time: bfloat16 [1152, 768], P('rows')
- grad_space: bfloat16 [3456, 192], P('rows')
The draws below stay inside these ranges and needn't reach their ends.
All inputs are finite; a program needn't handle non-finite values.
Results may differ from the reference program's by a relative error of at most 0.025.
Values may be sent and summed in bfloat16 or wider, within the bound.
No kernel may reach another device: no remote copies, remote signals or barrier semaphores. Data moves between devices by JAX's collectives and lax.ppermute only.
A program may use at most 64 MiB of HBM per device.

```python
import math
import jax
import jax.numpy as jnp
from jax import lax

C = 384
CH = 192
F = 2
R = 2
W = 48
CLIPS = 2
FR = 16
H = 64
VOXELS = 786432
N_CHAIN = 8
N_ROWS = 32
N_CLIP = 2


def spiked(drawn, key, source, target, blocks, factor):
    owner, partner = [(jnp.arange(drawn.shape[position]) // (drawn.shape[position] // blocks)).reshape([-1 if axis == position else 1 for axis in range(drawn.ndim)]) for position in (source, target)]
    chosen = jax.random.permutation(key, blocks)[partner]
    strong = (owner == chosen) | (owner == (partner + blocks // 2) % blocks)
    return jnp.where(strong, factor * drawn, drawn)


def steps_of(key, shape, cuts, smallest, top_value):
    gain = 1.0
    for dim, blocks in cuts:
        steps = jax.random.uniform(jax.random.fold_in(jax.random.fold_in(key, 6), dim), (blocks,), jnp.float32, smallest / len(cuts), top_value / len(cuts))
        gain = gain * jnp.repeat(jnp.exp(steps), shape[dim] // blocks).reshape((-1,) + (1,) * (len(shape) - 1 - dim))
    return gain


def noise(own_key, extent, spread, limit, shards=(), kind=jnp.bfloat16):
    array = spread * jax.random.normal(own_key, extent, jnp.float32)
    if shards:
        array = array * steps_of(own_key, extent, shards, -0.22, 0.18)
    return jnp.clip(array, -limit, limit).astype(kind)


def gaussian_with(stream_key, dims, width, reach, cuts, heavy, kind=jnp.bfloat16):
    array = width * jax.random.normal(stream_key, dims, jnp.float32)
    if cuts:
        array = array * steps_of(stream_key, dims, cuts, -0.22, 0.18)
    return jnp.clip(spiked(array, jax.random.fold_in(stream_key, 3), *heavy), -reach, reach).astype(kind)


def setup_inputs(seed: int = 0) -> dict:
    arg_keys = jax.random.split(jax.random.key(seed), 5)
    return {
        "video": gaussian_with(arg_keys[0], (CLIPS, FR, H, W, C), 1.0, 6.0, ((0, 2), (1, 8), (2, 32)), (2, 4, 32, 2.75)),
        "cotangent": noise(arg_keys[1], (CLIPS, 2 * FR, 2 * H, 2 * W, CH), 1.0, 6.0, ((0, 2), (1, 8), (2, 32))),
        "w_time": noise(arg_keys[2], (3, C, 2 * C), (3 * C) ** -0.5, 0.1875),
        "w_space": noise(arg_keys[3], (3, 3, C, CH), (9 * C) ** -0.5, 0.109375),
    }


def time_conv(extended, w_time, frames):
    channels = extended.shape[-1]
    summed_taps = jnp.zeros((frames * extended.shape[1] * extended.shape[2], w_time.shape[2]), jnp.float32)
    for tap_t in range(3):
        summed_taps = summed_taps + jnp.dot(extended[tap_t:tap_t + frames].reshape(-1, channels), w_time[tap_t], preferred_element_type=jnp.float32)
    return summed_taps.astype(jnp.bfloat16).reshape(frames, extended.shape[1], extended.shape[2], w_time.shape[2])

def backward_block(hidden, own_input, padded_cot, w_time, w_space):
    frames, rows_ext, columns, doubled = hidden.shape
    band_rows = rows_ext - 2
    channels = doubled // 2
    half_ch = w_space.shape[3]
    upsampled = hidden.reshape(frames, rows_ext, columns, 2, channels).transpose(0, 3, 1, 2, 4).reshape(2 * frames, rows_ext, columns, channels)
    upsampled = jnp.repeat(jnp.repeat(upsampled, 2, axis=1), 2, axis=2)[:, 1:2 * band_rows + 3]
    upsampled = jnp.pad(upsampled, ((0, 0), (0, 0), (1, 1), (0, 0)))
    cot_core = padded_cot[:, 1:2 * band_rows + 1, 1:2 * columns + 1].reshape(-1, half_ch)
    space_terms = []
    grad_up = jnp.zeros((8 * frames * band_rows * columns, channels), jnp.float32)
    for tap_r in range(3):
        for tap_c in range(3):
            window = upsampled[:, tap_r:tap_r + 2 * band_rows, tap_c:tap_c + 2 * columns].reshape(-1, channels)
            space_terms.append(jnp.dot(window.T, cot_core, preferred_element_type=jnp.float32))
            shifted = padded_cot[:, 2 - tap_r:2 - tap_r + 2 * band_rows, 2 - tap_c:2 - tap_c + 2 * columns].reshape(-1, half_ch)
            grad_up = grad_up + jnp.dot(shifted, w_space[tap_r, tap_c].T, preferred_element_type=jnp.float32)
    part_space = jnp.stack(space_terms).reshape(9 * channels, half_ch)
    summed = grad_up.reshape(2 * frames, band_rows, 2, columns, 2, channels).sum(axis=(2, 4))
    grad_hidden = summed.reshape(frames, 2, band_rows, columns, channels).transpose(0, 2, 3, 1, 4).reshape(frames * band_rows * columns, 2 * channels).astype(jnp.bfloat16)
    time_terms = []
    for tap_t in range(3):
        time_terms.append(jnp.dot(own_input[tap_t:tap_t + frames].reshape(-1, channels).T, grad_hidden, preferred_element_type=jnp.float32))
    part_time = jnp.stack(time_terms).reshape(3 * channels, 2 * channels)
    grad_ext = jnp.zeros((frames + 2, band_rows, columns, channels), jnp.float32)
    for tap_t in range(3):
        grad_ext = grad_ext.at[tap_t:tap_t + frames].add(jnp.dot(grad_hidden, w_time[tap_t].T, preferred_element_type=jnp.float32).reshape(frames, band_rows, columns, channels))
    return (part_time, part_space, grad_ext)

def reference(video, cotangent, w_time, w_space):
    padded_video = jnp.pad(video, ((0, 0), (2, 0), (1, 1), (0, 0), (0, 0)))
    padded_cot = jnp.pad(cotangent, ((0, 0), (0, 0), (1, 1), (1, 1), (0, 0)))
    blocks = N_CLIP * N_CHAIN * N_ROWS
    anchor = jnp.zeros((), jnp.int32)

    def accumulate(running, block_id):
        acc_time, acc_space, grad_acc = running
        clip_id = (block_id // (N_CHAIN * N_ROWS)).astype(jnp.int32)
        frame_id = (block_id // N_ROWS % N_CHAIN).astype(jnp.int32)
        band_id = (block_id % N_ROWS).astype(jnp.int32)
        rimmed = lax.dynamic_slice(padded_video, (clip_id, frame_id * F, band_id * R, anchor, anchor), (1, F + 2, R + 2, W, C))[0]
        cot_block = lax.dynamic_slice(padded_cot, (clip_id, frame_id * 2 * F, band_id * 2 * R, anchor, anchor), (1, 2 * F, 2 * R + 2, 2 * W + 2, CH))[0]
        hidden = time_conv(rimmed, w_time, F)
        part_time, part_space, grad_ext = backward_block(hidden, rimmed[:, 1:R + 1], cot_block, w_time, w_space)
        rounded_time = lax.optimization_barrier(part_time.astype(jnp.bfloat16))
        rounded_space = lax.optimization_barrier(part_space.astype(jnp.bfloat16))
        acc_time = acc_time + rounded_time.astype(jnp.float32)
        acc_space = acc_space + rounded_space.astype(jnp.float32)
        starts = (clip_id, frame_id * F, band_id * R, anchor, anchor)
        region = lax.dynamic_slice(grad_acc, starts, (1, F + 2, R, W, C))
        grad_acc = lax.dynamic_update_slice(grad_acc, region + grad_ext[None], starts)
        return ((acc_time, acc_space, grad_acc), None)
    initial = (jnp.zeros((3 * C, 2 * C), jnp.float32), jnp.zeros((9 * C, CH), jnp.float32), jnp.zeros((CLIPS, FR + 2, H, W, C), jnp.float32))
    final, unused = lax.scan(accumulate, initial, jnp.arange(blocks, dtype=jnp.int32))
    acc_time, acc_space, grad_acc = final
    grad_scale = 1.0 / math.sqrt(VOXELS)
    grad_video = grad_acc[:, 2:].astype(jnp.bfloat16)
    return (grad_video, (acc_time * grad_scale).astype(jnp.bfloat16), (acc_space * grad_scale).astype(jnp.bfloat16))
```

```python
import math

import jax
import jax.numpy as jnp
from jax import lax
from jax.experimental import pallas as pl
from jax.experimental.pallas import tpu as pltpu
from jax.sharding import PartitionSpec as P

FRAMES, BAND, COLS, CH_IN, CH_OUT = 2, 2, 48, 384, 192
CELLS = BAND * COLS
N_X, N_Z = 4, 8
F32, BF16 = jnp.float32, jnp.bfloat16
LANES = 128
PIECE = 24
TIME_ROWS, SPACE_ROWS = 36, 108


def dot(a, b):
    return jnp.dot(a, b, preferred_element_type=F32)


def dot_t(a, b):
    return lax.dot_general(a, b, (((0,), (0,)), ((), ())), preferred_element_type=F32)


def block_kernel(cot, low, high, video, carried, w_time, w_space, packed, grad_hidden, ext, z, hid, time_acc, space_acc, line):
    ext[0 : FRAMES * CELLS] = carried[...]
    ext[FRAMES * CELLS :] = video[...]

    row = lax.broadcasted_iota(jnp.int32, (3 * COLS, 2 * COLS), 0)
    col = lax.broadcasted_iota(jnp.int32, (3 * COLS, 2 * COLS), 1)
    first = 2 * (row % COLS) + 1 - row // COLS
    pick = jnp.where((col == first) | (col == first + 1), 1.0, 0.0).astype(BF16)
    for s in range(2 * FRAMES):
        reach = [dot(pick, low[s])]
        for p in range(2 * BAND):
            reach.append(dot(pick, cot[s, p]))
        reach.append(dot(pick, high[s]))
        pairs = [(reach[i] + reach[i + 1]).astype(BF16) for i in range(2 * BAND + 1)]
        for p in range(BAND):
            for a in range(3):
                both = pairs[2 * p + 2 - a]
                for c in range(3):
                    start = s * CELLS + p * COLS
                    z[3 * a + c, start : start + COLS] = both[c * COLS : (c + 1) * COLS]

    grad = dot(z[0], w_space[0])
    for tap in range(1, 9):
        grad = grad + dot(z[tap], w_space[tap])
    for t in range(FRAMES):
        for j in range(2):
            s = 2 * t + j
            grad_hidden[t * CELLS : (t + 1) * CELLS, j * CH_IN : (j + 1) * CH_IN] = grad[
                s * CELLS : (s + 1) * CELLS
            ].astype(BF16)

    hidden = dot(ext[0 : FRAMES * CELLS], w_time[0])
    for k in range(1, 3):
        hidden = hidden + dot(ext[k * CELLS : (k + FRAMES) * CELLS], w_time[k])
    for t in range(FRAMES):
        for j in range(2):
            s = 2 * t + j
            hid[s * CELLS : (s + 1) * CELLS] = hidden[
                t * CELLS : (t + 1) * CELLS, j * CH_IN : (j + 1) * CH_IN
            ].astype(BF16)

    for k in range(3):
        time_acc[k * CH_IN : (k + 1) * CH_IN] = dot_t(ext[k * CELLS : (k + FRAMES) * CELLS], grad_hidden[...])
    hid_t = hid[...].T
    for tap in range(9):
        space_acc[tap * CH_IN : (tap + 1) * CH_IN] = dot(hid_t, z[tap])

    line[378:384] = jnp.zeros((6, LANES), F32)
    half = SPACE_ROWS // 2
    for r in range(N_X * N_Z):
        t0, s0 = r * TIME_ROWS, r * SPACE_ROWS
        for j in range(6):
            line[j * TIME_ROWS : (j + 1) * TIME_ROWS] = time_acc[t0 : t0 + TIME_ROWS, j * LANES : (j + 1) * LANES]
        line[216:324] = space_acc[s0 : s0 + SPACE_ROWS, 0:LANES]
        line[324:378] = jnp.concatenate(
            [space_acc[s0 : s0 + half, LANES:CH_OUT], space_acc[s0 + half : s0 + SPACE_ROWS, LANES:CH_OUT]], axis=1
        )
        for piece in range(16):
            packed[piece % 2, r // N_Z, piece // 2, r % N_Z] = line[piece * PIECE : (piece + 1) * PIECE].astype(BF16)


def block_terms(cot, low, high, video, carried, w_time, w_space):
    cells = FRAMES * CELLS
    return pl.pallas_call(
        block_kernel,
        name="block_terms",
        out_shape=(
            jax.ShapeDtypeStruct((2, N_X, 8, N_Z, PIECE, LANES), BF16),
            jax.ShapeDtypeStruct((cells, 2 * CH_IN), BF16),
        ),
        in_specs=[pl.BlockSpec(memory_space=pltpu.VMEM)] * 7,
        out_specs=(pl.BlockSpec(memory_space=pltpu.VMEM),) * 2,
        scratch_shapes=[
            pltpu.VMEM((2 * cells, CH_IN), BF16),
            pltpu.VMEM((9, 2 * cells, CH_OUT), BF16),
            pltpu.VMEM((2 * cells, CH_IN), BF16),
            pltpu.VMEM((3 * CH_IN, 2 * CH_IN), F32),
            pltpu.VMEM((9 * CH_IN, CH_OUT), F32),
            pltpu.VMEM((16 * PIECE, LANES), F32),
        ],
        compiler_params=pltpu.CompilerParams(vmem_limit_bytes=40 * 1024 * 1024),
    )(cot, low, high, video, carried, w_time, w_space)


def video_kernel(own, following, w_time, out):
    ahead = jnp.concatenate([own[...], following[...]], axis=0)
    total = None
    for k in range(3):
        term = lax.dot_general(
            ahead[(2 - k) * CELLS : (2 - k + FRAMES) * CELLS],
            w_time[k],
            (((1,), (1,)), ((), ())),
            preferred_element_type=F32,
        )
        total = term if total is None else total + term
    out[...] = total.astype(BF16)


def video_grad(own, following, w_time):
    return pl.pallas_call(
        video_kernel,
        name="video_grad",
        out_shape=jax.ShapeDtypeStruct((FRAMES * CELLS, CH_IN), BF16),
        in_specs=[pl.BlockSpec(memory_space=pltpu.VMEM)] * 3,
        out_specs=pl.BlockSpec(memory_space=pltpu.VMEM),
        compiler_params=pltpu.CompilerParams(vmem_limit_bytes=16 * 1024 * 1024),
    )(own, following, w_time)


def unpack(lines):
    time = lines[:216].reshape(6, TIME_ROWS, LANES).transpose(1, 0, 2).reshape(TIME_ROWS, 6 * LANES)
    rest = lines[324:378]
    space = jnp.concatenate([lines[216:324], jnp.concatenate([rest[:, :64], rest[:, 64:]], axis=0)], axis=1)
    return time, space


def along(axis, steps):
    count = lax.axis_size(axis)
    return [(i, i + steps) for i in range(count) if 0 <= i + steps < count]


def local(video, cotangent, w_time, w_space):
    cot = cotangent[0]
    own = video[0].reshape(FRAMES * CELLS, CH_IN)
    rows, chain = lax.axis_size("rows"), lax.axis_size("chain")
    low = lax.ppermute(cot[:, 2 * BAND - 1], "rows", along("rows", 1))
    high = lax.ppermute(cot[:, 0], "rows", along("rows", -1))
    carried = lax.ppermute(own, "chain", along("chain", 1))
    packed, grad_hidden = block_terms(
        cot, low, high, own, carried, w_time, w_space.transpose(0, 1, 3, 2).reshape(9, CH_OUT, CH_IN)
    )
    following = lax.ppermute(grad_hidden, "chain", along("chain", -1))

    share = packed.reshape(2, -1, LANES)
    share = lax.all_to_all(share, "clip", 0, 0, tiled=True)
    share = share.astype(F32).sum(0).astype(BF16)
    across_x = [[x * N_Z + z for x in range(N_X)] for z in range(N_Z)]
    share = lax.all_to_all(share.reshape(N_X, -1, LANES), "rows", 0, 0, tiled=True, axis_index_groups=across_x)
    share = share.astype(F32).sum(0).astype(BF16)
    across_cz = [[c * rows + x * N_Z + z for c in range(chain) for z in range(N_Z)] for x in range(N_X)]
    share = lax.all_to_all(
        share.reshape(chain * N_Z, PIECE, LANES), ("chain", "rows"), 0, 0, tiled=True, axis_index_groups=across_cz
    )
    voxels = 2 * chain * 2 * FRAMES * rows * 2 * BAND * 2 * COLS
    piece = (share.astype(F32).sum(0) * (1.0 / math.sqrt(voxels))).astype(BF16)
    pieces = jnp.broadcast_to(piece[None], (2 * chain, PIECE, LANES))
    pieces = lax.all_to_all(pieces, ("chain", "clip"), 0, 0, tiled=True)
    grad_time, grad_space = unpack(pieces.reshape(2 * chain * PIECE, LANES))
    grad_video = video_grad(grad_hidden, following, w_time).reshape(video.shape)
    return grad_video, grad_time, grad_space


def solution(mesh):
    placed = P("clip", "chain", "rows", None, None)
    return jax.shard_map(
        local,
        mesh=mesh,
        in_specs=(placed, placed, P(), P()),
        out_specs=(placed, P("rows", None), P("rows", None)),
        check_vma=False,
    )
```

```python
import math

import jax
import jax.numpy as jnp
from jax import lax
from jax.experimental import pallas as pl
from jax.experimental.pallas import tpu as pltpu
from jax.sharding import PartitionSpec as P

FRAMES, BAND, COLS, CH_IN, CH_OUT = 2, 2, 48, 384, 192
CELLS = BAND * COLS
N_X, N_Z = 4, 8
F32, BF16 = jnp.float32, jnp.bfloat16
LANES = 128
PIECE, LINES = 48, 384
TIME_ROWS, SPACE_ROWS = 36, 108


def dot(a, b):
    return jnp.dot(a, b, preferred_element_type=F32)


def dot_t(a, b):
    return lax.dot_general(a, b, (((0,), (0,)), ((), ())), preferred_element_type=F32)


VMEM = pl.BlockSpec(memory_space=pltpu.VMEM)


def params(mib):
    return pltpu.CompilerParams(vmem_limit_bytes=mib * 1024 * 1024)


def picker():
    row = lax.broadcasted_iota(jnp.int32, (3 * COLS, 2 * COLS), 0)
    col = lax.broadcasted_iota(jnp.int32, (3 * COLS, 2 * COLS), 1)
    first = 2 * (row % COLS) + 1 - row // COLS
    return jnp.where((col == first) | (col == first + 1), 1.0, 0.0).astype(BF16)


def put(z, a, p, s, both):
    start = (p * 2 * FRAMES + s) * COLS
    for c in range(3):
        z[3 * a + c, start : start + COLS] = both[c * COLS : (c + 1) * COLS]


HALF = 2 * FRAMES * COLS


def edges_kernel(cot, top, bottom, sems):
    copies = [
        pltpu.make_async_copy(cot.at[:, 2 * BAND - 1], bottom, sems.at[0]),
        pltpu.make_async_copy(cot.at[:, 0], top, sems.at[1]),
    ]
    for copy in copies:
        copy.start()
    for copy in copies:
        copy.wait()


def edges(cot):
    edge = jax.ShapeDtypeStruct((2 * FRAMES, 2 * COLS, CH_OUT), BF16)
    return pl.pallas_call(
        edges_kernel,
        name="edges",
        out_shape=(edge, edge),
        in_specs=[pl.BlockSpec(memory_space=pl.ANY)],
        out_specs=(VMEM, VMEM),
        scratch_shapes=[pltpu.SemaphoreType.DMA((2,))],
    )(cot)


def inner_kernel(cot, video, w_time, w_space, z, grad, hidden):
    pick = picker()
    for s in range(2 * FRAMES):
        reach = [dot(pick, cot[s, p]) for p in range(2 * BAND)]
        for p in range(BAND):
            put(z, 1, p, s, (reach[2 * p] + reach[2 * p + 1]).astype(BF16))
        both = (reach[1] + reach[2]).astype(BF16)
        put(z, 0, 0, s, both)
        put(z, 2, 1, s, both)
    total = dot(z[3], w_space[3])
    for tap in (4, 5):
        total = total + dot(z[tap], w_space[tap])
    upper, lower = total[:HALF], total[HALF:]
    for c in range(3):
        upper = upper + dot(z[c, :HALF], w_space[c])
        lower = lower + dot(z[6 + c, HALF:], w_space[6 + c])
    grad[:HALF] = upper
    grad[HALF:] = lower
    hidden[:CELLS] = dot(video[:CELLS], w_time[2])
    hidden[CELLS:] = dot(video[:CELLS], w_time[1]) + dot(video[CELLS:], w_time[2])


def inner_terms(cot, video, w_time, w_space):
    cells = FRAMES * CELLS
    return pl.pallas_call(
        inner_kernel,
        name="inner_terms",
        out_shape=(
            jax.ShapeDtypeStruct((9, 2 * cells, CH_OUT), BF16),
            jax.ShapeDtypeStruct((2 * cells, CH_IN), F32),
            jax.ShapeDtypeStruct((cells, 2 * CH_IN), F32),
        ),
        in_specs=[VMEM] * 4,
        out_specs=(VMEM,) * 3,
        compiler_params=params(12),
        cost_estimate=pl.CostEstimate(flops=1_500_000_000, bytes_accessed=6_000_000, transcendentals=0),
    )(cot, video, w_time, w_space)


def block_kernel(
    cot, low, high, video, carried, w_time, w_space, z_in, grad_in, hidden_in,
    keep, send, grad_hidden, z,
    ext, hid, time_acc, space_acc, line,
):
    ext[0 : FRAMES * CELLS] = carried[...]
    ext[FRAMES * CELLS :] = video[...]
    pick = picker()
    for s in range(2 * FRAMES):
        put(z, 2, 0, s, (dot(pick, low[s]) + dot(pick, cot[s, 0])).astype(BF16))
        put(z, 0, 1, s, (dot(pick, cot[s, 2 * BAND - 1]) + dot(pick, high[s])).astype(BF16))
    upper, lower = grad_in[:HALF], grad_in[HALF:]
    for c in range(3):
        upper = upper + dot(z[6 + c, :HALF], w_space[6 + c])
        lower = lower + dot(z[c, HALF:], w_space[c])
    for p, part in enumerate((upper, lower)):
        for t in range(FRAMES):
            for j in range(2):
                s = 2 * t + j
                grad_hidden[(t * BAND + p) * COLS : (t * BAND + p + 1) * COLS, j * CH_IN : (j + 1) * CH_IN] = part[
                    s * COLS : (s + 1) * COLS
                ].astype(BF16)

    first = hidden_in[:CELLS] + dot(carried[:CELLS], w_time[0]) + dot(carried[CELLS:], w_time[1])
    second = hidden_in[CELLS:] + dot(carried[CELLS:], w_time[0])
    for t, hidden in enumerate((first, second)):
        for p in range(BAND):
            for j in range(2):
                start = (p * 2 * FRAMES + 2 * t + j) * COLS
                hid[start : start + COLS] = hidden[
                    p * COLS : (p + 1) * COLS, j * CH_IN : (j + 1) * CH_IN
                ].astype(BF16)

    for k in range(3):
        time_acc[k * CH_IN : (k + 1) * CH_IN] = dot_t(ext[k * CELLS : (k + FRAMES) * CELLS], grad_hidden[...])
    hid_t = hid[...].T
    for tap in range(9):
        space_acc[tap * CH_IN : (tap + 1) * CH_IN] = dot(hid_t, z[tap])

    mine = lax.axis_index("clip")
    line[378:LINES] = jnp.zeros((6, LANES), F32)
    half = SPACE_ROWS // 2
    for r in range(N_X * N_Z):
        x, zh, zl = r // N_Z, r % N_Z // 2, r % 2
        t0, s0 = r * TIME_ROWS, r * SPACE_ROWS
        for j in range(6):
            line[j * TIME_ROWS : (j + 1) * TIME_ROWS] = time_acc[t0 : t0 + TIME_ROWS, j * LANES : (j + 1) * LANES]
        line[216:324] = space_acc[s0 : s0 + SPACE_ROWS, 0:LANES]
        line[324:378] = jnp.concatenate(
            [space_acc[s0 : s0 + half, LANES:CH_OUT], space_acc[s0 + half : s0 + SPACE_ROWS, LANES:CH_OUT]], axis=1
        )
        for c0 in range(2):
            for c1 in range(2):
                piece = (c0 * 2 + c1) * PIECE
                own = pl.multiple_of(mine * (LINES // 2) + piece, 8)
                other = pl.multiple_of((1 - mine) * (LINES // 2) + piece, 8)
                keep[x, c0, zl, c1, zh] = line[pl.ds(own, PIECE)].astype(BF16)
                send[x, c0, zl, c1, zh] = line[pl.ds(other, PIECE)].astype(BF16)


def block_terms(cot, low, high, video, carried, w_time, w_space, z, grad, hidden):
    cells = FRAMES * CELLS
    half = jax.ShapeDtypeStruct((N_X, 2, 2, 2, N_Z // 2, PIECE, LANES), BF16)
    return pl.pallas_call(
        block_kernel,
        name="block_terms",
        out_shape=(
            half,
            half,
            jax.ShapeDtypeStruct((cells, 2 * CH_IN), BF16),
            jax.ShapeDtypeStruct(z.shape, BF16),
        ),
        in_specs=[VMEM] * 10,
        out_specs=(VMEM,) * 4,
        input_output_aliases={7: 3},
        scratch_shapes=[
            pltpu.VMEM((2 * cells, CH_IN), BF16),
            pltpu.VMEM((2 * cells, CH_IN), BF16),
            pltpu.VMEM((3 * CH_IN, 2 * CH_IN), F32),
            pltpu.VMEM((9 * CH_IN, CH_OUT), F32),
            pltpu.VMEM((LINES, LANES), F32),
        ],
        compiler_params=params(24),
        cost_estimate=pl.CostEstimate(flops=2_500_000_000, bytes_accessed=10_000_000, transcendentals=0),
    )(cot, low, high, video, carried, w_time, w_space, z, grad, hidden)


def pair_kernel(a, b, out):
    out[...] = (a[...].astype(F32) + b[...].astype(F32)).astype(BF16)


def pair_sum(a, b):
    return pl.pallas_call(
        pair_kernel,
        name="pair_sum",
        out_shape=jax.ShapeDtypeStruct(a.shape, BF16),
        in_specs=[VMEM] * 2,
        out_specs=VMEM,
        compiler_params=params(8),
    )(a, b)


def group_kernel(copies, parts, out):
    total = parts[0].astype(F32)
    for i in range(1, parts.shape[0]):
        total = total + parts[i].astype(F32)
    total = total.astype(BF16)
    if copies is None:
        out[...] = total
    else:
        for i in range(copies):
            out[i] = total


def group_sum(parts, copies=None):
    lead = () if copies is None else (copies,)
    return pl.pallas_call(
        lambda *refs: group_kernel(copies, *refs),
        name="group_sum",
        out_shape=jax.ShapeDtypeStruct(lead + parts.shape[1:], BF16),
        in_specs=[VMEM],
        out_specs=VMEM,
        compiler_params=params(8),
    )(parts)


def unpack_kernel(scale, pieces, time, space, line):
    for k in range(2):
        for c0 in range(2):
            for c1 in range(2):
                low = (c1 * 2 + c0) * 2 + k
                start = ((k * 2 + c0) * 2 + c1) * PIECE
                total = pieces[low].astype(F32) + pieces[8 + low].astype(F32)
                line[start : start + PIECE] = total * scale
    for j in range(6):
        time[:, j * LANES : (j + 1) * LANES] = line[j * TIME_ROWS : (j + 1) * TIME_ROWS].astype(BF16)
    space[0:LANES] = line[216 : 216 + LANES].T[:, :SPACE_ROWS].astype(BF16)
    half = SPACE_ROWS // 2
    rest = line[324 : 324 + 64].T
    space[LANES:] = jnp.concatenate([rest[0:64, :half], rest[64:, :half]], axis=1).astype(BF16)


def unpack(pieces, scale):
    return pl.pallas_call(
        lambda *refs: unpack_kernel(scale, *refs),
        name="unpack",
        out_shape=(
            jax.ShapeDtypeStruct((TIME_ROWS, 6 * LANES), BF16),
            jax.ShapeDtypeStruct((CH_OUT, SPACE_ROWS), BF16),
        ),
        in_specs=[VMEM],
        out_specs=(VMEM, VMEM),
        scratch_shapes=[pltpu.VMEM((LINES + 8, LANES), F32)],
        compiler_params=params(8),
    )(pieces)


def video_kernel(own, following, w_time, out):
    ahead = jnp.concatenate([own[...], following[...]], axis=0)
    total = None
    for k in range(3):
        term = lax.dot_general(
            ahead[(2 - k) * CELLS : (2 - k + FRAMES) * CELLS],
            w_time[k],
            (((1,), (1,)), ((), ())),
            preferred_element_type=F32,
        )
        total = term if total is None else total + term
    out[...] = total.astype(BF16)


def video_grad(own, following, w_time):
    return pl.pallas_call(
        video_kernel,
        name="video_grad",
        out_shape=jax.ShapeDtypeStruct((FRAMES * CELLS, CH_IN), BF16),
        in_specs=[VMEM] * 3,
        out_specs=VMEM,
        compiler_params=params(8),
        cost_estimate=pl.CostEstimate(flops=350_000_000, bytes_accessed=2_500_000, transcendentals=0),
    )(own, following, w_time)


def along(axis, steps):
    count = lax.axis_size(axis)
    return [(i, i + steps) for i in range(count) if 0 <= i + steps < count]


def exchange(parts, groups):
    return lax.all_to_all(parts, ("chain", "rows"), 0, 0, tiled=True, axis_index_groups=groups)


def local(video, cotangent, w_time, w_space):
    cot = cotangent[0]
    own = video[0].reshape(FRAMES * CELLS, CH_IN)
    rows, chain = lax.axis_size("rows"), lax.axis_size("chain")
    w_space = w_space.transpose(0, 1, 3, 2).reshape(9, CH_OUT, CH_IN)
    top, bottom = edges(cot)
    low = lax.ppermute(bottom, "rows", along("rows", 1))
    high = lax.ppermute(top, "rows", along("rows", -1))
    carried = lax.ppermute(own, "chain", along("chain", 1))
    inner = inner_terms(cot, own, w_time, w_space)
    keep, send, grad_hidden, _ = block_terms(cot, low, high, own, carried, w_time, w_space, *inner)
    received = lax.ppermute(send, "clip", [(0, 1), (1, 0)])
    following = lax.ppermute(grad_hidden, "chain", along("chain", -1))

    def device(c, x, z):
        return c * rows + x * N_Z + z

    near = [
        [device(2 * ch + c, x, 2 * zh + z) for x in range(N_X) for c in range(2) for z in range(2)]
        for ch in range(chain // 2)
        for zh in range(N_Z // 2)
    ]
    far = [
        [device(4 * c2 + 2 * c + c0, x, 2 * zh + zl) for c in range(2) for zh in range(N_Z // 2)]
        for c2 in range(chain // 4)
        for c0 in range(2)
        for x in range(N_X)
        for zl in range(2)
    ]
    share = pair_sum(keep.reshape(-1, LANES), received.reshape(-1, LANES))
    share = group_sum(exchange(share.reshape(4 * N_X, -1, LANES), near))
    share = group_sum(exchange(share.reshape(N_Z, PIECE, LANES), far), 2 * chain)
    pieces = lax.all_to_all(share, ("chain", "clip"), 0, 0, tiled=True)
    voxels = 2 * chain * 2 * FRAMES * rows * 2 * BAND * 2 * COLS
    grad_time, grad_space = unpack(pieces, 1.0 / math.sqrt(voxels))
    grad_video = video_grad(grad_hidden, following, w_time).reshape(video.shape)
    return grad_video, grad_time, grad_space.T


def solution(mesh):
    placed = P("clip", "chain", "rows", None, None)
    return jax.shard_map(
        local,
        mesh=mesh,
        in_specs=(placed, placed, P(), P()),
        out_specs=(placed, P("rows", None), P("rows", None)),
        check_vma=False,
    )
```

```python
import math

import jax
import jax.numpy as jnp
from jax import lax
from jax.experimental import pallas as pl
from jax.experimental.pallas import tpu as pltpu
from jax.sharding import PartitionSpec as P

FRAMES, BAND, COLS, CH_IN, CH_OUT = 2, 2, 48, 384, 192
CELLS = BAND * COLS
N_X, N_Z = 4, 8
F32, BF16 = jnp.float32, jnp.bfloat16
LANES = 128
PIECE, LINES = 48, 384
TIME_ROWS, SPACE_ROWS = 36, 108


def dot(a, b):
    return jnp.dot(a, b, preferred_element_type=F32)


def dot_t(a, b):
    return lax.dot_general(a, b, (((0,), (0,)), ((), ())), preferred_element_type=F32)


VMEM = pl.BlockSpec(memory_space=pltpu.VMEM)


def params(mib):
    return pltpu.CompilerParams(vmem_limit_bytes=mib * 1024 * 1024)


def picker():
    row = lax.broadcasted_iota(jnp.int32, (3 * COLS, 2 * COLS), 0)
    col = lax.broadcasted_iota(jnp.int32, (3 * COLS, 2 * COLS), 1)
    first = 2 * (row % COLS) + 1 - row // COLS
    return jnp.where((col == first) | (col == first + 1), 1.0, 0.0).astype(BF16)


HALF = 2 * FRAMES * COLS


def put(z, row, s, both):
    for c in range(3):
        z[row + c, s * COLS : (s + 1) * COLS] = both[c * COLS : (c + 1) * COLS]


INNER, OUTER = ((0, 1), (1, 1), (0, 0), (1, 2)), ((0, 2), (1, 0))


def taps(z, which, w_space):
    sums = [0.0, 0.0]
    for i, (p, a) in enumerate(which):
        for c in range(3):
            sums[p] = sums[p] + dot(z[3 * i + c], w_space[3 * a + c])
    return sums


def inner_kernel(cot_in, video_in, w_time_in, w_space_in, cot, video, w_time, w_space, inner, grad, hidden, sems):
    copies = [
        pltpu.make_async_copy(source, target, sems.at[i])
        for i, (source, target) in enumerate(
            ((cot_in, cot), (w_space_in, w_space), (video_in, video), (w_time_in, w_time))
        )
    ]
    for copy in copies:
        copy.start()
    pick = picker()
    copies[0].wait()
    for s in range(2 * FRAMES):
        reach = [dot(pick, cot[s, p]) for p in range(2 * BAND)]
        for i, (p, a) in enumerate(INNER):
            put(inner, 3 * i, s, (reach[2 * p + 1 - a] + reach[2 * p + 2 - a]).astype(BF16))
    copies[1].wait()
    grad[...] = jnp.concatenate(taps(inner, INNER, w_space))
    copies[2].wait()
    copies[3].wait()
    hidden[:CELLS] = dot(video[:CELLS], w_time[2])
    hidden[CELLS:] = dot(video[:CELLS], w_time[1]) + dot(video[CELLS:], w_time[2])


def inner_terms(cot, video, w_time, w_space):
    cells = FRAMES * CELLS
    return pl.pallas_call(
        inner_kernel,
        name="inner_terms",
        out_shape=(
            *(jax.ShapeDtypeStruct(array.shape, BF16) for array in (cot, video, w_time, w_space)),
            jax.ShapeDtypeStruct((3 * len(INNER), HALF, CH_OUT), BF16),
            jax.ShapeDtypeStruct((2 * cells, CH_IN), F32),
            jax.ShapeDtypeStruct((cells, 2 * CH_IN), F32),
        ),
        in_specs=[pl.BlockSpec(memory_space=pltpu.HBM)] * 4,
        out_specs=(VMEM,) * 7,
        scratch_shapes=[pltpu.SemaphoreType.DMA((4,))],
        compiler_params=params(16),
        cost_estimate=pl.CostEstimate(flops=1_500_000_000, bytes_accessed=6_000_000, transcendentals=0),
    )(cot, video, w_time, w_space)


def grad_kernel(cot, low, high, w_space, grad_in, grad_hidden, outer):
    pick = picker()
    for s in range(2 * FRAMES):
        put(outer, 0, s, (dot(pick, low[s, 0]) + dot(pick, cot[s, 0])).astype(BF16))
        put(outer, 3, s, (dot(pick, cot[s, 2 * BAND - 1]) + dot(pick, high[s, 0])).astype(BF16))
    for p, part in enumerate(taps(outer, OUTER, w_space)):
        part = part + grad_in[p * HALF : (p + 1) * HALF]
        for t in range(FRAMES):
            for j in range(2):
                s = 2 * t + j
                grad_hidden[(t * BAND + p) * COLS : (t * BAND + p + 1) * COLS, j * CH_IN : (j + 1) * CH_IN] = part[
                    s * COLS : (s + 1) * COLS
                ].astype(BF16)


def grad_terms(cot, low, high, w_space, grad):
    return pl.pallas_call(
        grad_kernel,
        name="grad_terms",
        out_shape=(
            jax.ShapeDtypeStruct((FRAMES * CELLS, 2 * CH_IN), BF16),
            jax.ShapeDtypeStruct((3 * len(OUTER), HALF, CH_OUT), BF16),
        ),
        in_specs=[VMEM] * 5,
        out_specs=(VMEM,) * 2,
        compiler_params=params(8),
        cost_estimate=pl.CostEstimate(flops=800_000_000, bytes_accessed=4_000_000, transcendentals=0),
    )(cot, low, high, w_space, grad)


def block_kernel(
    video, carried, w_time, inner, outer, grad_hidden, hidden_in,
    keep, send,
    ext, hid, time_acc, space_acc, line,
):
    ext[0 : FRAMES * CELLS] = carried[...]
    ext[FRAMES * CELLS :] = video[...]
    first = hidden_in[:CELLS] + dot(carried[:CELLS], w_time[0]) + dot(carried[CELLS:], w_time[1])
    second = hidden_in[CELLS:] + dot(carried[CELLS:], w_time[0])
    for t, hidden in enumerate((first, second)):
        for p in range(BAND):
            for j in range(2):
                start = (p * 2 * FRAMES + 2 * t + j) * COLS
                hid[start : start + COLS] = hidden[
                    p * COLS : (p + 1) * COLS, j * CH_IN : (j + 1) * CH_IN
                ].astype(BF16)

    for k in range(3):
        time_acc[k * CH_IN : (k + 1) * CH_IN] = dot_t(ext[k * CELLS : (k + FRAMES) * CELLS], grad_hidden[...])
    hid_t = [hid[p * HALF : (p + 1) * HALF].T for p in range(BAND)]
    where = {key: (z, 3 * i) for z, order in ((inner, INNER), (outer, OUTER)) for i, key in enumerate(order)}
    for a in range(3):
        for c in range(3):
            total = 0.0
            for p in range(BAND):
                z, row = where[p, a]
                total = total + dot(hid_t[p], z[row + c])
            tap = 3 * a + c
            space_acc[tap * CH_IN : (tap + 1) * CH_IN] = total

    mine = lax.axis_index("clip")
    line[378:LINES] = jnp.zeros((6, LANES), F32)
    half = SPACE_ROWS // 2
    for r in range(N_X * N_Z):
        x, zh, zl = r // N_Z, r % N_Z // 2, r % 2
        t0, s0 = r * TIME_ROWS, r * SPACE_ROWS
        for j in range(6):
            line[j * TIME_ROWS : (j + 1) * TIME_ROWS] = time_acc[t0 : t0 + TIME_ROWS, j * LANES : (j + 1) * LANES]
        line[216:324] = space_acc[s0 : s0 + SPACE_ROWS, 0:LANES]
        line[324:378] = jnp.concatenate(
            [space_acc[s0 : s0 + half, LANES:CH_OUT], space_acc[s0 + half : s0 + SPACE_ROWS, LANES:CH_OUT]], axis=1
        )
        for c0 in range(2):
            for c1 in range(2):
                piece = (c0 * 2 + c1) * PIECE
                own = pl.multiple_of(mine * (LINES // 2) + piece, 8)
                other = pl.multiple_of((1 - mine) * (LINES // 2) + piece, 8)
                keep[x, c0, zl, c1, zh] = line[pl.ds(own, PIECE)].astype(BF16)
                send[x, c0, zl, c1, zh] = line[pl.ds(other, PIECE)].astype(BF16)


def block_terms(video, carried, w_time, inner, outer, grad_hidden, hidden):
    cells = FRAMES * CELLS
    half = jax.ShapeDtypeStruct((N_X, 2, 2, 2, N_Z // 2, PIECE, LANES), BF16)
    return pl.pallas_call(
        block_kernel,
        name="block_terms",
        out_shape=(half, half),
        in_specs=[VMEM] * 7,
        out_specs=(VMEM,) * 2,
        scratch_shapes=[
            pltpu.VMEM((2 * cells, CH_IN), BF16),
            pltpu.VMEM((2 * cells, CH_IN), BF16),
            pltpu.VMEM((3 * CH_IN, 2 * CH_IN), F32),
            pltpu.VMEM((9 * CH_IN, CH_OUT), F32),
            pltpu.VMEM((LINES, LANES), F32),
        ],
        compiler_params=params(20),
        cost_estimate=pl.CostEstimate(flops=3_000_000_000, bytes_accessed=12_000_000, transcendentals=0),
    )(video, carried, w_time, inner, outer, grad_hidden, hidden)


def pair_kernel(a, b, out):
    out[...] = (a[...].astype(F32) + b[...].astype(F32)).astype(BF16)


def pair_sum(a, b):
    return pl.pallas_call(
        pair_kernel,
        name="pair_sum",
        out_shape=jax.ShapeDtypeStruct(a.shape, BF16),
        in_specs=[VMEM] * 2,
        out_specs=VMEM,
        compiler_params=params(8),
    )(a, b)


def group_kernel(copies, parts, out):
    total = parts[0].astype(F32)
    for i in range(1, parts.shape[0]):
        total = total + parts[i].astype(F32)
    total = total.astype(BF16)
    if copies is None:
        out[...] = total
    else:
        for i in range(copies):
            out[i] = total


def group_sum(parts, copies=None):
    lead = () if copies is None else (copies,)
    return pl.pallas_call(
        lambda *refs: group_kernel(copies, *refs),
        name="group_sum",
        out_shape=jax.ShapeDtypeStruct(lead + parts.shape[1:], BF16),
        in_specs=[VMEM],
        out_specs=VMEM,
        compiler_params=params(8),
    )(parts)


def unpack_kernel(scale, pieces, time, space, line):
    for k in range(2):
        for c0 in range(2):
            for c1 in range(2):
                low = (c1 * 2 + c0) * 2 + k
                start = ((k * 2 + c0) * 2 + c1) * PIECE
                total = pieces[low].astype(F32) + pieces[8 + low].astype(F32)
                line[start : start + PIECE] = total * scale
    for j in range(6):
        time[:, j * LANES : (j + 1) * LANES] = line[j * TIME_ROWS : (j + 1) * TIME_ROWS].astype(BF16)
    space[0:LANES] = line[216 : 216 + LANES].T[:, :SPACE_ROWS].astype(BF16)
    half = SPACE_ROWS // 2
    rest = line[324 : 324 + 64].T
    space[LANES:] = jnp.concatenate([rest[0:64, :half], rest[64:, :half]], axis=1).astype(BF16)


def unpack(pieces, scale):
    return pl.pallas_call(
        lambda *refs: unpack_kernel(scale, *refs),
        name="unpack",
        out_shape=(
            jax.ShapeDtypeStruct((TIME_ROWS, 6 * LANES), BF16),
            jax.ShapeDtypeStruct((CH_OUT, SPACE_ROWS), BF16),
        ),
        in_specs=[VMEM],
        out_specs=(VMEM, VMEM),
        scratch_shapes=[pltpu.VMEM((LINES + 8, LANES), F32)],
        compiler_params=params(8),
    )(pieces)


def video_kernel(own, following, w_time, out):
    ahead = jnp.concatenate([own[...], following[...]], axis=0)
    total = None
    for k in range(3):
        term = lax.dot_general(
            ahead[(2 - k) * CELLS : (2 - k + FRAMES) * CELLS],
            w_time[k],
            (((1,), (1,)), ((), ())),
            preferred_element_type=F32,
        )
        total = term if total is None else total + term
    out[...] = total.astype(BF16)


def video_grad(own, following, w_time):
    return pl.pallas_call(
        video_kernel,
        name="video_grad",
        out_shape=jax.ShapeDtypeStruct((FRAMES * CELLS, CH_IN), BF16),
        in_specs=[VMEM] * 3,
        out_specs=VMEM,
        compiler_params=params(8),
        cost_estimate=pl.CostEstimate(flops=350_000_000, bytes_accessed=2_500_000, transcendentals=0),
    )(own, following, w_time)


def along(axis, steps):
    count = lax.axis_size(axis)
    return [(i, i + steps) for i in range(count) if 0 <= i + steps < count]


def exchange(parts, groups):
    return lax.all_to_all(parts, ("chain", "rows"), 0, 0, tiled=True, axis_index_groups=groups)


def local(video, cotangent, w_time, w_space):
    cot = cotangent[0]
    own = video[0].reshape(FRAMES * CELLS, CH_IN)
    rows, chain = lax.axis_size("rows"), lax.axis_size("chain")
    w_space = w_space.transpose(0, 1, 3, 2).reshape(9, CH_OUT, CH_IN)
    low = lax.ppermute(cot[:, 2 * BAND - 1 :], "rows", along("rows", 1))
    high = lax.ppermute(cot[:, :1], "rows", along("rows", -1))
    carried = lax.ppermute(own, "chain", along("chain", 1))
    operands = [pltpu.with_memory_space_constraint(value, pltpu.HBM) for value in (cot, own, w_time, w_space)]
    cot, own, w_time, w_space, inner, grad, hidden = inner_terms(*operands)
    grad_hidden, outer = grad_terms(cot, low, high, w_space, grad)
    following = lax.ppermute(grad_hidden, "chain", along("chain", -1))
    keep, send = block_terms(own, carried, w_time, inner, outer, grad_hidden, hidden)
    received = lax.ppermute(send, "clip", [(0, 1), (1, 0)])
    received, following = lax.optimization_barrier((received, following))

    def device(c, x, z):
        return c * rows + x * N_Z + z

    near = [
        [device(2 * ch + c, x, 2 * zh + z) for x in range(N_X) for c in range(2) for z in range(2)]
        for ch in range(chain // 2)
        for zh in range(N_Z // 2)
    ]
    far = [
        [device(4 * c2 + 2 * c + c0, x, 2 * zh + zl) for c in range(2) for zh in range(N_Z // 2)]
        for c2 in range(chain // 4)
        for c0 in range(2)
        for x in range(N_X)
        for zl in range(2)
    ]
    share = pair_sum(keep.reshape(-1, LANES), received.reshape(-1, LANES))
    share = group_sum(exchange(share.reshape(4 * N_X, -1, LANES), near))
    share = group_sum(exchange(share.reshape(N_Z, PIECE, LANES), far), 2 * chain)
    pieces = lax.all_to_all(share, ("chain", "clip"), 0, 0, tiled=True)
    voxels = 2 * chain * 2 * FRAMES * rows * 2 * BAND * 2 * COLS
    grad_time, grad_space = unpack(pieces, 1.0 / math.sqrt(voxels))
    grad_video = video_grad(grad_hidden, following, w_time).reshape(video.shape)
    return grad_video, grad_time, grad_space.T


def solution(mesh):
    placed = P("clip", "chain", "rows", None, None)
    return jax.shard_map(
        local,
        mesh=mesh,
        in_specs=(placed, placed, P(), P()),
        out_specs=(placed, P("rows", None), P("rows", None)),
        check_vma=False,
    )
```

```python
import math

import jax
import jax.numpy as jnp
from jax import lax
from jax.experimental import pallas as pl
from jax.experimental.pallas import tpu as pltpu
from jax.sharding import PartitionSpec as P

FRAMES, BAND, COLS, CH_IN, CH_OUT = 2, 2, 48, 384, 192
CELLS = BAND * COLS
N_X, N_Z = 4, 8
F32, BF16 = jnp.float32, jnp.bfloat16
LANES = 128
PIECE, LINES = 48, 384
TIME_ROWS, SPACE_ROWS = 36, 108


def dot(a, b):
    return jnp.dot(a, b, preferred_element_type=F32)


def dot_t(a, b):
    return lax.dot_general(a, b, (((0,), (0,)), ((), ())), preferred_element_type=F32)


VMEM = pl.BlockSpec(memory_space=pltpu.VMEM)


def params(mib):
    return pltpu.CompilerParams(vmem_limit_bytes=mib * 1024 * 1024)


def picker():
    row = lax.broadcasted_iota(jnp.int32, (3 * COLS, 2 * COLS), 0)
    col = lax.broadcasted_iota(jnp.int32, (3 * COLS, 2 * COLS), 1)
    first = 2 * (row % COLS) + 1 - row // COLS
    return jnp.where((col == first) | (col == first + 1), 1.0, 0.0).astype(BF16)


HALF = 2 * FRAMES * COLS


def put(z, row, s, both):
    for c in range(3):
        z[row + c, s * COLS : (s + 1) * COLS] = both[c * COLS : (c + 1) * COLS]


INNER, OUTER = ((0, 1), (1, 1), (0, 0), (1, 2)), ((0, 2), (1, 0))


def taps(z, which, w_space):
    sums = [0.0, 0.0]
    for i, (p, a) in enumerate(which):
        for c in range(3):
            sums[p] = sums[p] + dot(z[3 * i + c], w_space[3 * a + c])
    return sums


def inner_kernel(cot_in, video_in, w_time_in, w_space_in, cot, video, w_time, w_space, inner, grad, hidden, sems):
    copies = [
        pltpu.make_async_copy(source, target, sems.at[i])
        for i, (source, target) in enumerate(
            ((cot_in, cot), (w_space_in, w_space), (video_in, video), (w_time_in, w_time))
        )
    ]
    for copy in copies:
        copy.start()
    pick = picker()
    copies[0].wait()
    for s in range(2 * FRAMES):
        reach = [dot(pick, cot[s, p]) for p in range(2 * BAND)]
        for i, (p, a) in enumerate(INNER):
            put(inner, 3 * i, s, (reach[2 * p + 1 - a] + reach[2 * p + 2 - a]).astype(BF16))
    copies[1].wait()
    grad[...] = jnp.concatenate(taps(inner, INNER, w_space))
    copies[2].wait()
    copies[3].wait()
    hidden[:CELLS] = dot(video[:CELLS], w_time[2])
    hidden[CELLS:] = dot(video[:CELLS], w_time[1]) + dot(video[CELLS:], w_time[2])


def inner_terms(cot, video, w_time, w_space):
    cells = FRAMES * CELLS
    return pl.pallas_call(
        inner_kernel,
        name="inner_terms",
        out_shape=(
            *(jax.ShapeDtypeStruct(array.shape, BF16) for array in (cot, video, w_time, w_space)),
            jax.ShapeDtypeStruct((3 * len(INNER), HALF, CH_OUT), BF16),
            jax.ShapeDtypeStruct((2 * cells, CH_IN), F32),
            jax.ShapeDtypeStruct((cells, 2 * CH_IN), F32),
        ),
        in_specs=[pl.BlockSpec(memory_space=pltpu.HBM)] * 4,
        out_specs=(VMEM,) * 7,
        scratch_shapes=[pltpu.SemaphoreType.DMA((4,))],
        compiler_params=params(16),
        cost_estimate=pl.CostEstimate(flops=1_500_000_000, bytes_accessed=6_000_000, transcendentals=0),
    )(cot, video, w_time, w_space)


def grad_kernel(cot, low, high, w_space, grad_in, grad_hidden, outer):
    pick = picker()
    for s in range(2 * FRAMES):
        put(outer, 0, s, (dot(pick, low[s, 0]) + dot(pick, cot[s, 0])).astype(BF16))
        put(outer, 3, s, (dot(pick, cot[s, 2 * BAND - 1]) + dot(pick, high[s, 0])).astype(BF16))
    for p, part in enumerate(taps(outer, OUTER, w_space)):
        part = part + grad_in[p * HALF : (p + 1) * HALF]
        for t in range(FRAMES):
            for j in range(2):
                s = 2 * t + j
                grad_hidden[(t * BAND + p) * COLS : (t * BAND + p + 1) * COLS, j * CH_IN : (j + 1) * CH_IN] = part[
                    s * COLS : (s + 1) * COLS
                ].astype(BF16)


def grad_terms(cot, low, high, w_space, grad):
    return pl.pallas_call(
        grad_kernel,
        name="grad_terms",
        out_shape=(
            jax.ShapeDtypeStruct((FRAMES * CELLS, 2 * CH_IN), BF16),
            jax.ShapeDtypeStruct((3 * len(OUTER), HALF, CH_OUT), BF16),
        ),
        in_specs=[VMEM] * 5,
        out_specs=(VMEM,) * 2,
        compiler_params=params(8),
        cost_estimate=pl.CostEstimate(flops=800_000_000, bytes_accessed=4_000_000, transcendentals=0),
    )(cot, low, high, w_space, grad)


def block_kernel(
    video, carried, w_time, inner, outer, grad_hidden, hidden_in,
    keep, send,
    ext, hid, time_acc, space_acc, line,
):
    ext[0 : FRAMES * CELLS] = carried[...]
    ext[FRAMES * CELLS :] = video[...]
    first = hidden_in[:CELLS] + dot(carried[:CELLS], w_time[0]) + dot(carried[CELLS:], w_time[1])
    second = hidden_in[CELLS:] + dot(carried[CELLS:], w_time[0])
    for t, hidden in enumerate((first, second)):
        for p in range(BAND):
            for j in range(2):
                start = (p * 2 * FRAMES + 2 * t + j) * COLS
                hid[start : start + COLS] = hidden[
                    p * COLS : (p + 1) * COLS, j * CH_IN : (j + 1) * CH_IN
                ].astype(BF16)

    for k in range(3):
        time_acc[k * CH_IN : (k + 1) * CH_IN] = dot_t(ext[k * CELLS : (k + FRAMES) * CELLS], grad_hidden[...])
    hid_t = [hid[p * HALF : (p + 1) * HALF].T for p in range(BAND)]
    where = {key: (z, 3 * i) for z, order in ((inner, INNER), (outer, OUTER)) for i, key in enumerate(order)}
    for a in range(3):
        for c in range(3):
            total = 0.0
            for p in range(BAND):
                z, row = where[p, a]
                total = total + dot(hid_t[p], z[row + c])
            tap = 3 * a + c
            space_acc[tap * CH_IN : (tap + 1) * CH_IN] = total

    mine = lax.axis_index("clip")
    line[378:LINES] = jnp.zeros((6, LANES), F32)
    half = SPACE_ROWS // 2
    for r in range(N_X * N_Z):
        x, zh, zl = r // N_Z, r % N_Z // 2, r % 2
        t0, s0 = r * TIME_ROWS, r * SPACE_ROWS
        for j in range(6):
            line[j * TIME_ROWS : (j + 1) * TIME_ROWS] = time_acc[t0 : t0 + TIME_ROWS, j * LANES : (j + 1) * LANES]
        line[216:324] = space_acc[s0 : s0 + SPACE_ROWS, 0:LANES]
        line[324:378] = jnp.concatenate(
            [space_acc[s0 : s0 + half, LANES:CH_OUT], space_acc[s0 + half : s0 + SPACE_ROWS, LANES:CH_OUT]], axis=1
        )
        for c0 in range(2):
            for c1 in range(2):
                piece = (c0 * 2 + c1) * PIECE
                own = pl.multiple_of(mine * (LINES // 2) + piece, 8)
                other = pl.multiple_of((1 - mine) * (LINES // 2) + piece, 8)
                keep[x, c0, zl, c1, zh] = line[pl.ds(own, PIECE)].astype(BF16)
                send[x, c0, zl, c1, zh] = line[pl.ds(other, PIECE)].astype(BF16)


def block_terms(video, carried, w_time, inner, outer, grad_hidden, hidden):
    cells = FRAMES * CELLS
    half = jax.ShapeDtypeStruct((N_X, 2, 2, 2, N_Z // 2, PIECE, LANES), BF16)
    return pl.pallas_call(
        block_kernel,
        name="block_terms",
        out_shape=(half, half),
        in_specs=[VMEM] * 7,
        out_specs=(VMEM,) * 2,
        scratch_shapes=[
            pltpu.VMEM((2 * cells, CH_IN), BF16),
            pltpu.VMEM((2 * cells, CH_IN), BF16),
            pltpu.VMEM((3 * CH_IN, 2 * CH_IN), F32),
            pltpu.VMEM((9 * CH_IN, CH_OUT), F32),
            pltpu.VMEM((LINES, LANES), F32),
        ],
        compiler_params=params(20),
        cost_estimate=pl.CostEstimate(flops=3_000_000_000, bytes_accessed=12_000_000, transcendentals=0),
    )(video, carried, w_time, inner, outer, grad_hidden, hidden)


def pair_kernel(a, b, out):
    out[...] = (a[...].astype(F32) + b[...].astype(F32)).astype(BF16)


def pair_sum(a, b):
    return pl.pallas_call(
        pair_kernel,
        name="pair_sum",
        out_shape=jax.ShapeDtypeStruct(a.shape, BF16),
        in_specs=[VMEM] * 2,
        out_specs=VMEM,
        compiler_params=params(8),
    )(a, b)


def group_kernel(copies, parts, out):
    total = parts[0].astype(F32)
    for i in range(1, parts.shape[0]):
        total = total + parts[i].astype(F32)
    total = total.astype(BF16)
    if copies is None:
        out[...] = total
    else:
        for i in range(copies):
            out[i] = total


def group_sum(parts, copies=None):
    lead = () if copies is None else (copies,)
    return pl.pallas_call(
        lambda *refs: group_kernel(copies, *refs),
        name="group_sum",
        out_shape=jax.ShapeDtypeStruct(lead + parts.shape[1:], BF16),
        in_specs=[VMEM],
        out_specs=VMEM,
        compiler_params=params(8),
    )(parts)


def unpack_kernel(scale, pieces, time, space, line):
    for k in range(2):
        for c0 in range(2):
            for c1 in range(2):
                low = (c1 * 2 + c0) * 2 + k
                start = ((k * 2 + c0) * 2 + c1) * PIECE
                total = pieces[low].astype(F32) + pieces[8 + low].astype(F32)
                line[start : start + PIECE] = total * scale
    for j in range(6):
        time[:, j * LANES : (j + 1) * LANES] = line[j * TIME_ROWS : (j + 1) * TIME_ROWS].astype(BF16)
    space[0:LANES] = line[216 : 216 + LANES].T[:, :SPACE_ROWS].astype(BF16)
    half = SPACE_ROWS // 2
    rest = line[324 : 324 + 64].T
    space[LANES:] = jnp.concatenate([rest[0:64, :half], rest[64:, :half]], axis=1).astype(BF16)


def unpack(pieces, scale):
    return pl.pallas_call(
        lambda *refs: unpack_kernel(scale, *refs),
        name="unpack",
        out_shape=(
            jax.ShapeDtypeStruct((TIME_ROWS, 6 * LANES), BF16),
            jax.ShapeDtypeStruct((CH_OUT, SPACE_ROWS), BF16),
        ),
        in_specs=[VMEM],
        out_specs=(VMEM, VMEM),
        scratch_shapes=[pltpu.VMEM((LINES + 8, LANES), F32)],
        compiler_params=params(8),
    )(pieces)


def video_kernel(own, following, w_time, out):
    ahead = jnp.concatenate([own[...], following[...]], axis=0)
    total = None
    for k in range(3):
        term = lax.dot_general(
            ahead[(2 - k) * CELLS : (2 - k + FRAMES) * CELLS],
            w_time[k],
            (((1,), (1,)), ((), ())),
            preferred_element_type=F32,
        )
        total = term if total is None else total + term
    out[...] = total.astype(BF16)


def video_grad(own, following, w_time):
    return pl.pallas_call(
        video_kernel,
        name="video_grad",
        out_shape=jax.ShapeDtypeStruct((FRAMES * CELLS, CH_IN), BF16),
        in_specs=[VMEM] * 3,
        out_specs=VMEM,
        compiler_params=params(8),
        cost_estimate=pl.CostEstimate(flops=350_000_000, bytes_accessed=2_500_000, transcendentals=0),
    )(own, following, w_time)


def along(axis, steps):
    count = lax.axis_size(axis)
    return [(i, i + steps) for i in range(count) if 0 <= i + steps < count]


def exchange(parts, groups):
    return lax.all_to_all(parts, ("chain", "rows"), 0, 0, tiled=True, axis_index_groups=groups)


def local(video, cotangent, w_time, w_space):
    cot = cotangent[0]
    own = video[0].reshape(FRAMES * CELLS, CH_IN)
    rows, chain = lax.axis_size("rows"), lax.axis_size("chain")
    w_space = w_space.transpose(0, 1, 3, 2).reshape(9, CH_OUT, CH_IN)
    low = lax.ppermute(cot[:, 2 * BAND - 1 :], "rows", along("rows", 1))
    high = lax.ppermute(cot[:, :1], "rows", along("rows", -1))
    carried = lax.ppermute(own, "chain", along("chain", 1))
    operands = [pltpu.with_memory_space_constraint(value, pltpu.HBM) for value in (cot, own, w_time, w_space)]
    cot, own, w_time, w_space, inner, grad, hidden = inner_terms(*operands)
    grad_hidden, outer = grad_terms(cot, low, high, w_space, grad)
    following = lax.ppermute(grad_hidden, "chain", along("chain", -1))
    keep, send = block_terms(own, carried, w_time, inner, outer, grad_hidden, hidden)
    received = lax.ppermute(send, "clip", [(0, 1), (1, 0)])

    def device(c, x, z):
        return c * rows + x * N_Z + z

    near = [
        [device(2 * ch + c, x, 2 * zh + z) for x in range(N_X) for c in range(2) for z in range(2)]
        for ch in range(chain // 2)
        for zh in range(N_Z // 2)
    ]
    far = [
        [device(4 * c2 + 2 * c + c0, x, 2 * zh + zl) for c in range(2) for zh in range(N_Z // 2)]
        for c2 in range(chain // 4)
        for c0 in range(2)
        for x in range(N_X)
        for zl in range(2)
    ]
    share = pair_sum(keep.reshape(-1, LANES), received.reshape(-1, LANES))
    share, following = lax.optimization_barrier((exchange(share.reshape(4 * N_X, -1, LANES), near), following))
    share = group_sum(share)
    share = group_sum(exchange(share.reshape(N_Z, PIECE, LANES), far), 2 * chain)
    pieces = lax.all_to_all(share, ("chain", "clip"), 0, 0, tiled=True)
    voxels = 2 * chain * 2 * FRAMES * rows * 2 * BAND * 2 * COLS
    grad_time, grad_space = unpack(pieces, 1.0 / math.sqrt(voxels))
    grad_video = video_grad(grad_hidden, following, w_time).reshape(video.shape)
    return grad_video, grad_time, grad_space.T


def solution(mesh):
    placed = P("clip", "chain", "rows", None, None)
    return jax.shard_map(
        local,
        mesh=mesh,
        in_specs=(placed, placed, P(), P()),
        out_specs=(placed, P("rows", None), P("rows", None)),
        check_vma=False,
    )
```

```python
import math

import jax
import jax.numpy as jnp
from jax import lax
from jax.experimental import pallas as pl
from jax.experimental.pallas import tpu as pltpu
from jax.sharding import PartitionSpec as P

FRAMES, BAND, COLS, CH_IN, CH_OUT = 2, 2, 48, 384, 192
CELLS = BAND * COLS
N_X, N_Z = 4, 8
F32, BF16 = jnp.float32, jnp.bfloat16
LANES = 128
PIECE, LINES = 48, 384
TIME_ROWS, SPACE_ROWS = 36, 108


def dot(a, b):
    return jnp.dot(a, b, preferred_element_type=F32)


def dot_t(a, b):
    return lax.dot_general(a, b, (((0,), (0,)), ((), ())), preferred_element_type=F32)


VMEM = pl.BlockSpec(memory_space=pltpu.VMEM)


def params(mib):
    return pltpu.CompilerParams(vmem_limit_bytes=mib * 1024 * 1024)


def picker():
    row = lax.broadcasted_iota(jnp.int32, (3 * COLS, 2 * COLS), 0)
    col = lax.broadcasted_iota(jnp.int32, (3 * COLS, 2 * COLS), 1)
    first = 2 * (row % COLS) + 1 - row // COLS
    return jnp.where((col == first) | (col == first + 1), 1.0, 0.0).astype(BF16)


HALF = 2 * FRAMES * COLS


def put(z, row, s, both):
    for c in range(3):
        z[row + c, s * COLS : (s + 1) * COLS] = both[c * COLS : (c + 1) * COLS]


INNER, OUTER = ((0, 1), (1, 1), (0, 0), (1, 2)), ((0, 2), (1, 0))


def taps(z, which, w_space):
    sums = [0.0, 0.0]
    for i, (p, a) in enumerate(which):
        for c in range(3):
            sums[p] = sums[p] + dot(z[3 * i + c], w_space[3 * a + c])
    return sums


def inner_kernel(cot_in, video_in, w_time_in, w_space_in, cot, video, w_time, w_space, inner, grad, hidden, sems):
    copies = [
        pltpu.make_async_copy(source, target, sems.at[i])
        for i, (source, target) in enumerate(
            ((cot_in, cot), (w_space_in, w_space), (video_in, video), (w_time_in, w_time))
        )
    ]
    for copy in copies:
        copy.start()
    pick = picker()
    copies[0].wait()
    for s in range(2 * FRAMES):
        reach = [dot(pick, cot[s, p]) for p in range(2 * BAND)]
        for i, (p, a) in enumerate(INNER):
            put(inner, 3 * i, s, (reach[2 * p + 1 - a] + reach[2 * p + 2 - a]).astype(BF16))
    copies[1].wait()
    grad[...] = jnp.concatenate(taps(inner, INNER, w_space))
    copies[2].wait()
    copies[3].wait()
    hidden[:CELLS] = dot(video[:CELLS], w_time[2])
    hidden[CELLS:] = dot(video[:CELLS], w_time[1]) + dot(video[CELLS:], w_time[2])


def inner_terms(cot, video, w_time, w_space):
    cells = FRAMES * CELLS
    return pl.pallas_call(
        inner_kernel,
        name="inner_terms",
        out_shape=(
            *(jax.ShapeDtypeStruct(array.shape, BF16) for array in (cot, video, w_time, w_space)),
            jax.ShapeDtypeStruct((3 * len(INNER), HALF, CH_OUT), BF16),
            jax.ShapeDtypeStruct((2 * cells, CH_IN), F32),
            jax.ShapeDtypeStruct((cells, 2 * CH_IN), F32),
        ),
        in_specs=[pl.BlockSpec(memory_space=pltpu.HBM)] * 4,
        out_specs=(VMEM,) * 7,
        scratch_shapes=[pltpu.SemaphoreType.DMA((4,))],
        compiler_params=params(16),
        cost_estimate=pl.CostEstimate(flops=1_500_000_000, bytes_accessed=6_000_000, transcendentals=0),
    )(cot, video, w_time, w_space)


def grad_kernel(cot, low, high, w_space, grad_in, grad_hidden, outer):
    pick = picker()
    for s in range(2 * FRAMES):
        put(outer, 0, s, (dot(pick, low[s, 0]) + dot(pick, cot[s, 0])).astype(BF16))
        put(outer, 3, s, (dot(pick, cot[s, 2 * BAND - 1]) + dot(pick, high[s, 0])).astype(BF16))
    for p, part in enumerate(taps(outer, OUTER, w_space)):
        part = part + grad_in[p * HALF : (p + 1) * HALF]
        for t in range(FRAMES):
            for j in range(2):
                s = 2 * t + j
                grad_hidden[(t * BAND + p) * COLS : (t * BAND + p + 1) * COLS, j * CH_IN : (j + 1) * CH_IN] = part[
                    s * COLS : (s + 1) * COLS
                ].astype(BF16)


def grad_terms(cot, low, high, w_space, grad):
    return pl.pallas_call(
        grad_kernel,
        name="grad_terms",
        out_shape=(
            jax.ShapeDtypeStruct((FRAMES * CELLS, 2 * CH_IN), BF16),
            jax.ShapeDtypeStruct((3 * len(OUTER), HALF, CH_OUT), BF16),
        ),
        in_specs=[VMEM] * 5,
        out_specs=(VMEM,) * 2,
        compiler_params=params(8),
        cost_estimate=pl.CostEstimate(flops=800_000_000, bytes_accessed=4_000_000, transcendentals=0),
    )(cot, low, high, w_space, grad)


def block_kernel(
    video, carried, w_time, inner, outer, grad_hidden, hidden_in,
    keep, send,
    ext, hid, time_acc, space_acc, line,
):
    ext[0 : FRAMES * CELLS] = carried[...]
    ext[FRAMES * CELLS :] = video[...]
    first = hidden_in[:CELLS] + dot(carried[:CELLS], w_time[0]) + dot(carried[CELLS:], w_time[1])
    second = hidden_in[CELLS:] + dot(carried[CELLS:], w_time[0])
    for t, hidden in enumerate((first, second)):
        for p in range(BAND):
            for j in range(2):
                start = (p * 2 * FRAMES + 2 * t + j) * COLS
                hid[start : start + COLS] = hidden[
                    p * COLS : (p + 1) * COLS, j * CH_IN : (j + 1) * CH_IN
                ].astype(BF16)

    for k in range(3):
        time_acc[k * CH_IN : (k + 1) * CH_IN] = dot_t(ext[k * CELLS : (k + FRAMES) * CELLS], grad_hidden[...])
    hid_t = [hid[p * HALF : (p + 1) * HALF].T for p in range(BAND)]
    where = {key: (z, 3 * i) for z, order in ((inner, INNER), (outer, OUTER)) for i, key in enumerate(order)}
    for a in range(3):
        for c in range(3):
            total = 0.0
            for p in range(BAND):
                z, row = where[p, a]
                total = total + dot(hid_t[p], z[row + c])
            tap = 3 * a + c
            space_acc[tap * CH_IN : (tap + 1) * CH_IN] = total

    mine = lax.axis_index("clip")
    line[378:LINES] = jnp.zeros((6, LANES), F32)
    half = SPACE_ROWS // 2
    for r in range(N_X * N_Z):
        x, zh, zl = r // N_Z, r % N_Z // 2, r % 2
        t0, s0 = r * TIME_ROWS, r * SPACE_ROWS
        for j in range(6):
            line[j * TIME_ROWS : (j + 1) * TIME_ROWS] = time_acc[t0 : t0 + TIME_ROWS, j * LANES : (j + 1) * LANES]
        line[216:324] = space_acc[s0 : s0 + SPACE_ROWS, 0:LANES]
        line[324:378] = jnp.concatenate(
            [space_acc[s0 : s0 + half, LANES:CH_OUT], space_acc[s0 + half : s0 + SPACE_ROWS, LANES:CH_OUT]], axis=1
        )
        for c0 in range(2):
            for c1 in range(2):
                piece = (c0 * 2 + c1) * PIECE
                own = pl.multiple_of(mine * (LINES // 2) + piece, 8)
                other = pl.multiple_of((1 - mine) * (LINES // 2) + piece, 8)
                keep[x, c0, zl, c1, zh] = line[pl.ds(own, PIECE)].astype(BF16)
                send[x, c0, zl, c1, zh] = line[pl.ds(other, PIECE)].astype(BF16)


def block_terms(video, carried, w_time, inner, outer, grad_hidden, hidden):
    cells = FRAMES * CELLS
    half = jax.ShapeDtypeStruct((N_X, 2, 2, 2, N_Z // 2, PIECE, LANES), BF16)
    return pl.pallas_call(
        block_kernel,
        name="block_terms",
        out_shape=(half, half),
        in_specs=[VMEM] * 7,
        out_specs=(VMEM,) * 2,
        scratch_shapes=[
            pltpu.VMEM((2 * cells, CH_IN), BF16),
            pltpu.VMEM((2 * cells, CH_IN), BF16),
            pltpu.VMEM((3 * CH_IN, 2 * CH_IN), F32),
            pltpu.VMEM((9 * CH_IN, CH_OUT), F32),
            pltpu.VMEM((LINES, LANES), F32),
        ],
        compiler_params=params(20),
        cost_estimate=pl.CostEstimate(flops=3_000_000_000, bytes_accessed=12_000_000, transcendentals=0),
    )(video, carried, w_time, inner, outer, grad_hidden, hidden)


def pair_kernel(a, b, out):
    out[...] = (a[...].astype(F32) + b[...].astype(F32)).astype(BF16)


def pair_sum(a, b):
    return pl.pallas_call(
        pair_kernel,
        name="pair_sum",
        out_shape=jax.ShapeDtypeStruct(a.shape, BF16),
        in_specs=[VMEM] * 2,
        out_specs=VMEM,
        compiler_params=params(8),
    )(a, b)


def group_kernel(copies, parts, out):
    total = parts[0].astype(F32)
    for i in range(1, parts.shape[0]):
        total = total + parts[i].astype(F32)
    total = total.astype(BF16)
    if copies is None:
        out[...] = total
    else:
        for i in range(copies):
            out[i] = total


def group_sum(parts, copies=None):
    lead = () if copies is None else (copies,)
    return pl.pallas_call(
        lambda *refs: group_kernel(copies, *refs),
        name="group_sum",
        out_shape=jax.ShapeDtypeStruct(lead + parts.shape[1:], BF16),
        in_specs=[VMEM],
        out_specs=VMEM,
        compiler_params=params(8),
    )(parts)


def unpack_kernel(scale, pieces, time, space, line):
    for k in range(2):
        for c0 in range(2):
            for c1 in range(2):
                low = (c1 * 2 + c0) * 2 + k
                start = ((k * 2 + c0) * 2 + c1) * PIECE
                total = pieces[low].astype(F32) + pieces[8 + low].astype(F32)
                line[start : start + PIECE] = total * scale
    for j in range(6):
        time[:, j * LANES : (j + 1) * LANES] = line[j * TIME_ROWS : (j + 1) * TIME_ROWS].astype(BF16)
    space[0:LANES] = line[216 : 216 + LANES].T[:, :SPACE_ROWS].astype(BF16)
    half = SPACE_ROWS // 2
    rest = line[324 : 324 + 64].T
    space[LANES:] = jnp.concatenate([rest[0:64, :half], rest[64:, :half]], axis=1).astype(BF16)


def unpack(pieces, scale):
    return pl.pallas_call(
        lambda *refs: unpack_kernel(scale, *refs),
        name="unpack",
        out_shape=(
            jax.ShapeDtypeStruct((TIME_ROWS, 6 * LANES), BF16),
            jax.ShapeDtypeStruct((CH_OUT, SPACE_ROWS), BF16),
        ),
        in_specs=[VMEM],
        out_specs=(VMEM, VMEM),
        scratch_shapes=[pltpu.VMEM((LINES + 8, LANES), F32)],
        compiler_params=params(8),
    )(pieces)


def video_kernel(own, following, w_time, out):
    ahead = jnp.concatenate([own[...], following[...]], axis=0)
    total = None
    for k in range(3):
        term = lax.dot_general(
            ahead[(2 - k) * CELLS : (2 - k + FRAMES) * CELLS],
            w_time[k],
            (((1,), (1,)), ((), ())),
            preferred_element_type=F32,
        )
        total = term if total is None else total + term
    out[...] = total.astype(BF16)


def video_grad(own, following, w_time):
    return pl.pallas_call(
        video_kernel,
        name="video_grad",
        out_shape=jax.ShapeDtypeStruct((FRAMES * CELLS, CH_IN), BF16),
        in_specs=[VMEM] * 3,
        out_specs=VMEM,
        compiler_params=params(8),
        cost_estimate=pl.CostEstimate(flops=350_000_000, bytes_accessed=2_500_000, transcendentals=0),
    )(own, following, w_time)


def along(axis, steps):
    count = lax.axis_size(axis)
    return [(i, i + steps) for i in range(count) if 0 <= i + steps < count]


def exchange(parts, groups):
    return lax.all_to_all(parts, ("chain", "rows"), 0, 0, tiled=True, axis_index_groups=groups)


def local(video, cotangent, w_time, w_space):
    cot = cotangent[0]
    own = video[0].reshape(FRAMES * CELLS, CH_IN)
    rows, chain = lax.axis_size("rows"), lax.axis_size("chain")
    w_space = w_space.transpose(0, 1, 3, 2).reshape(9, CH_OUT, CH_IN)
    low = lax.ppermute(cot[:, 2 * BAND - 1 :], "rows", along("rows", 1))
    high = lax.ppermute(cot[:, :1], "rows", along("rows", -1))
    carried = lax.ppermute(own, "chain", along("chain", 1))
    operands = [pltpu.with_memory_space_constraint(value, pltpu.HBM) for value in (cot, own, w_time, w_space)]
    cot, own, w_time, w_space, inner, grad, hidden = inner_terms(*operands)
    grad_hidden, outer = grad_terms(cot, low, high, w_space, grad)
    keep, send = block_terms(own, carried, w_time, inner, outer, grad_hidden, hidden)
    received = lax.ppermute(send, "clip", [(0, 1), (1, 0)])

    def device(c, x, z):
        return c * rows + x * N_Z + z

    near = [
        [device(2 * ch + c, x, 2 * zh + z) for x in range(N_X) for c in range(2) for z in range(2)]
        for ch in range(chain // 2)
        for zh in range(N_Z // 2)
    ]
    far = [
        [device(4 * c2 + 2 * c + c0, x, 2 * zh + zl) for c in range(2) for zh in range(N_Z // 2)]
        for c2 in range(chain // 4)
        for c0 in range(2)
        for x in range(N_X)
        for zl in range(2)
    ]
    share = pair_sum(keep.reshape(-1, LANES), received.reshape(-1, LANES))
    share = group_sum(exchange(share.reshape(4 * N_X, -1, LANES), near))
    share, grad_hidden = lax.optimization_barrier((share, grad_hidden))
    following = lax.ppermute(grad_hidden, "chain", along("chain", -1))
    share, following = lax.optimization_barrier((exchange(share.reshape(N_Z, PIECE, LANES), far), following))
    share = group_sum(share, 2 * chain)
    pieces = lax.all_to_all(share, ("chain", "clip"), 0, 0, tiled=True)
    voxels = 2 * chain * 2 * FRAMES * rows * 2 * BAND * 2 * COLS
    grad_time, grad_space = unpack(pieces, 1.0 / math.sqrt(voxels))
    grad_video = video_grad(grad_hidden, following, w_time).reshape(video.shape)
    return grad_video, grad_time, grad_space.T


def solution(mesh):
    placed = P("clip", "chain", "rows", None, None)
    return jax.shard_map(
        local,
        mesh=mesh,
        in_specs=(placed, placed, P(), P()),
        out_specs=(placed, P("rows", None), P("rows", None)),
        check_vma=False,
    )
```

```python
import math

import jax
import jax.numpy as jnp
from jax import lax
from jax.experimental import pallas as pl
from jax.experimental.pallas import tpu as pltpu
from jax.sharding import PartitionSpec as P

FRAMES, BAND, COLS, CH_IN, CH_OUT = 2, 2, 48, 384, 192
CELLS = BAND * COLS
N_X, N_Z = 4, 8
F32, BF16 = jnp.float32, jnp.bfloat16
LANES = 128
PIECE, LINES = 48, 384
TIME_ROWS, SPACE_ROWS = 36, 108


def dot(a, b):
    return jnp.dot(a, b, preferred_element_type=F32)


def dot_rows(a, b):
    return lax.dot_general(a, b, (((1,), (1,)), ((), ())), preferred_element_type=F32)


def dot_t(a, b):
    return lax.dot_general(a, b, (((0,), (0,)), ((), ())), preferred_element_type=F32)


VMEM = pl.BlockSpec(memory_space=pltpu.VMEM)


def params(mib):
    return pltpu.CompilerParams(vmem_limit_bytes=mib * 1024 * 1024)


def picker():
    row = lax.broadcasted_iota(jnp.int32, (3 * COLS, 2 * COLS), 0)
    col = lax.broadcasted_iota(jnp.int32, (3 * COLS, 2 * COLS), 1)
    first = 2 * (row % COLS) + 1 - row // COLS
    return jnp.where((col == first) | (col == first + 1), 1.0, 0.0).astype(BF16)


HALF = 2 * FRAMES * COLS


def put(z, row, s, both):
    for c in range(3):
        z[row + c, s * COLS : (s + 1) * COLS] = both[c * COLS : (c + 1) * COLS]


INNER, OUTER = ((0, 1), (1, 1), (0, 0), (1, 2)), ((0, 2), (1, 0))


def taps(z, which, w_space):
    sums = [0.0, 0.0]
    for i, (p, a) in enumerate(which):
        for c in range(3):
            sums[p] = sums[p] + dot(z[3 * i + c], w_space[3 * a + c])
    return sums


def inner_kernel(cot_in, video_in, w_time_in, w_space_in, cot, video, w_time, w_space, inner, grad, hidden, sems):
    copies = [
        pltpu.make_async_copy(source, target, sems.at[i])
        for i, (source, target) in enumerate(
            ((cot_in, cot), (w_space_in, w_space), (video_in, video), (w_time_in, w_time))
        )
    ]
    for copy in copies:
        copy.start()
    pick = picker()
    copies[0].wait()
    for s in range(2 * FRAMES):
        reach = [dot(pick, cot[s, p]) for p in range(2 * BAND)]
        for i, (p, a) in enumerate(INNER):
            put(inner, 3 * i, s, (reach[2 * p + 1 - a] + reach[2 * p + 2 - a]).astype(BF16))
    copies[1].wait()
    grad[...] = jnp.concatenate(taps(inner, INNER, w_space))
    copies[2].wait()
    copies[3].wait()
    hidden[:CELLS] = dot(video[:CELLS], w_time[2])
    hidden[CELLS:] = dot(video[:CELLS], w_time[1]) + dot(video[CELLS:], w_time[2])


def inner_terms(cot, video, w_time, w_space):
    cells = FRAMES * CELLS
    return pl.pallas_call(
        inner_kernel,
        name="inner_terms",
        out_shape=(
            *(jax.ShapeDtypeStruct(array.shape, BF16) for array in (cot, video, w_time, w_space)),
            jax.ShapeDtypeStruct((3 * len(INNER), HALF, CH_OUT), BF16),
            jax.ShapeDtypeStruct((2 * cells, CH_IN), F32),
            jax.ShapeDtypeStruct((cells, 2 * CH_IN), F32),
        ),
        in_specs=[pl.BlockSpec(memory_space=pltpu.HBM)] * 4,
        out_specs=(VMEM,) * 7,
        scratch_shapes=[pltpu.SemaphoreType.DMA((4,))],
        compiler_params=params(16),
        cost_estimate=pl.CostEstimate(flops=1_500_000_000, bytes_accessed=6_000_000, transcendentals=0),
    )(cot, video, w_time, w_space)


def grad_kernel(cot, low, high, w_space, w_time, grad_in, grad_hidden, outer, returned):
    pick = picker()
    for s in range(2 * FRAMES):
        put(outer, 0, s, (dot(pick, low[s, 0]) + dot(pick, cot[s, 0])).astype(BF16))
        put(outer, 3, s, (dot(pick, cot[s, 2 * BAND - 1]) + dot(pick, high[s, 0])).astype(BF16))
    for p, part in enumerate(taps(outer, OUTER, w_space)):
        part = part + grad_in[p * HALF : (p + 1) * HALF]
        for t in range(FRAMES):
            for j in range(2):
                s = 2 * t + j
                grad_hidden[(t * BAND + p) * COLS : (t * BAND + p + 1) * COLS, j * CH_IN : (j + 1) * CH_IN] = part[
                    s * COLS : (s + 1) * COLS
                ].astype(BF16)
    first, second = grad_hidden[:CELLS], grad_hidden[CELLS:]
    returned[:CELLS] = dot_rows(first, w_time[0]).astype(BF16)
    returned[CELLS:] = (dot_rows(first, w_time[1]) + dot_rows(second, w_time[0])).astype(BF16)


def grad_terms(cot, low, high, w_space, w_time, grad):
    return pl.pallas_call(
        grad_kernel,
        name="grad_terms",
        out_shape=(
            jax.ShapeDtypeStruct((FRAMES * CELLS, 2 * CH_IN), BF16),
            jax.ShapeDtypeStruct((3 * len(OUTER), HALF, CH_OUT), BF16),
            jax.ShapeDtypeStruct((FRAMES * CELLS, CH_IN), BF16),
        ),
        in_specs=[VMEM] * 6,
        out_specs=(VMEM,) * 3,
        compiler_params=params(8),
        cost_estimate=pl.CostEstimate(flops=800_000_000, bytes_accessed=4_000_000, transcendentals=0),
    )(cot, low, high, w_space, w_time, grad)


def block_kernel(
    video, carried, w_time, inner, outer, grad_hidden, hidden_in,
    keep, send,
    ext, hid, time_acc, space_acc, line,
):
    ext[0 : FRAMES * CELLS] = carried[...]
    ext[FRAMES * CELLS :] = video[...]
    first = hidden_in[:CELLS] + dot(carried[:CELLS], w_time[0]) + dot(carried[CELLS:], w_time[1])
    second = hidden_in[CELLS:] + dot(carried[CELLS:], w_time[0])
    for t, hidden in enumerate((first, second)):
        for p in range(BAND):
            for j in range(2):
                start = (p * 2 * FRAMES + 2 * t + j) * COLS
                hid[start : start + COLS] = hidden[
                    p * COLS : (p + 1) * COLS, j * CH_IN : (j + 1) * CH_IN
                ].astype(BF16)

    for k in range(3):
        time_acc[k * CH_IN : (k + 1) * CH_IN] = dot_t(ext[k * CELLS : (k + FRAMES) * CELLS], grad_hidden[...])
    hid_t = [hid[p * HALF : (p + 1) * HALF].T for p in range(BAND)]
    where = {key: (z, 3 * i) for z, order in ((inner, INNER), (outer, OUTER)) for i, key in enumerate(order)}
    for a in range(3):
        for c in range(3):
            total = 0.0
            for p in range(BAND):
                z, row = where[p, a]
                total = total + dot(hid_t[p], z[row + c])
            tap = 3 * a + c
            space_acc[tap * CH_IN : (tap + 1) * CH_IN] = total

    mine = lax.axis_index("clip")
    line[378:LINES] = jnp.zeros((6, LANES), F32)
    half = SPACE_ROWS // 2
    for r in range(N_X * N_Z):
        x, zh, zl = r // N_Z, r % N_Z // 2, r % 2
        t0, s0 = r * TIME_ROWS, r * SPACE_ROWS
        for j in range(6):
            line[j * TIME_ROWS : (j + 1) * TIME_ROWS] = time_acc[t0 : t0 + TIME_ROWS, j * LANES : (j + 1) * LANES]
        line[216:324] = space_acc[s0 : s0 + SPACE_ROWS, 0:LANES]
        line[324:378] = jnp.concatenate(
            [space_acc[s0 : s0 + half, LANES:CH_OUT], space_acc[s0 + half : s0 + SPACE_ROWS, LANES:CH_OUT]], axis=1
        )
        for c0 in range(2):
            for c1 in range(2):
                piece = (c0 * 2 + c1) * PIECE
                own = pl.multiple_of(mine * (LINES // 2) + piece, 8)
                other = pl.multiple_of((1 - mine) * (LINES // 2) + piece, 8)
                keep[x, c0, zl, c1, zh] = line[pl.ds(own, PIECE)].astype(BF16)
                send[x, c0, zl, c1, zh] = line[pl.ds(other, PIECE)].astype(BF16)


def block_terms(video, carried, w_time, inner, outer, grad_hidden, hidden):
    cells = FRAMES * CELLS
    half = jax.ShapeDtypeStruct((N_X, 2, 2, 2, N_Z // 2, PIECE, LANES), BF16)
    return pl.pallas_call(
        block_kernel,
        name="block_terms",
        out_shape=(half, half),
        in_specs=[VMEM] * 7,
        out_specs=(VMEM,) * 2,
        scratch_shapes=[
            pltpu.VMEM((2 * cells, CH_IN), BF16),
            pltpu.VMEM((2 * cells, CH_IN), BF16),
            pltpu.VMEM((3 * CH_IN, 2 * CH_IN), F32),
            pltpu.VMEM((9 * CH_IN, CH_OUT), F32),
            pltpu.VMEM((LINES, LANES), F32),
        ],
        compiler_params=params(20),
        cost_estimate=pl.CostEstimate(flops=3_000_000_000, bytes_accessed=12_000_000, transcendentals=0),
    )(video, carried, w_time, inner, outer, grad_hidden, hidden)


def pair_kernel(a, b, out):
    out[...] = (a[...].astype(F32) + b[...].astype(F32)).astype(BF16)


def pair_sum(a, b):
    return pl.pallas_call(
        pair_kernel,
        name="pair_sum",
        out_shape=jax.ShapeDtypeStruct(a.shape, BF16),
        in_specs=[VMEM] * 2,
        out_specs=VMEM,
        compiler_params=params(8),
    )(a, b)


def group_kernel(copies, parts, out):
    total = parts[0].astype(F32)
    for i in range(1, parts.shape[0]):
        total = total + parts[i].astype(F32)
    total = total.astype(BF16)
    if copies is None:
        out[...] = total
    else:
        for i in range(copies):
            out[i] = total


def group_sum(parts, copies=None):
    lead = () if copies is None else (copies,)
    return pl.pallas_call(
        lambda *refs: group_kernel(copies, *refs),
        name="group_sum",
        out_shape=jax.ShapeDtypeStruct(lead + parts.shape[1:], BF16),
        in_specs=[VMEM],
        out_specs=VMEM,
        compiler_params=params(8),
    )(parts)


def unpack_kernel(scale, pieces, own, following, time, space, video, line):
    video[...] = (own[...] + following[...].astype(F32)).astype(BF16)
    for k in range(2):
        for c0 in range(2):
            for c1 in range(2):
                low = (c1 * 2 + c0) * 2 + k
                start = ((k * 2 + c0) * 2 + c1) * PIECE
                total = pieces[low].astype(F32) + pieces[8 + low].astype(F32)
                line[start : start + PIECE] = total * scale
    for j in range(6):
        time[:, j * LANES : (j + 1) * LANES] = line[j * TIME_ROWS : (j + 1) * TIME_ROWS].astype(BF16)
    space[0:LANES] = line[216 : 216 + LANES].T[:, :SPACE_ROWS].astype(BF16)
    half = SPACE_ROWS // 2
    rest = line[324 : 324 + 64].T
    space[LANES:] = jnp.concatenate([rest[0:64, :half], rest[64:, :half]], axis=1).astype(BF16)


def unpack(pieces, own, following, scale):
    return pl.pallas_call(
        lambda *refs: unpack_kernel(scale, *refs),
        name="unpack",
        out_shape=(
            jax.ShapeDtypeStruct((TIME_ROWS, 6 * LANES), BF16),
            jax.ShapeDtypeStruct((CH_OUT, SPACE_ROWS), BF16),
            jax.ShapeDtypeStruct(own.shape, BF16),
        ),
        in_specs=[VMEM] * 3,
        out_specs=(VMEM,) * 3,
        scratch_shapes=[pltpu.VMEM((LINES + 8, LANES), F32)],
        compiler_params=params(8),
    )(pieces, own, following)


def video_kernel(grad_hidden, w_time, out):
    first, second = grad_hidden[:CELLS], grad_hidden[CELLS:]
    out[:CELLS] = dot_rows(first, w_time[2]) + dot_rows(second, w_time[1])
    out[CELLS:] = dot_rows(second, w_time[2])


def video_terms(grad_hidden, w_time):
    return pl.pallas_call(
        video_kernel,
        name="video_terms",
        out_shape=jax.ShapeDtypeStruct((FRAMES * CELLS, CH_IN), F32),
        in_specs=[VMEM] * 2,
        out_specs=VMEM,
        compiler_params=params(8),
        cost_estimate=pl.CostEstimate(flops=350_000_000, bytes_accessed=2_500_000, transcendentals=0),
    )(grad_hidden, w_time)


def along(axis, steps):
    count = lax.axis_size(axis)
    return [(i, i + steps) for i in range(count) if 0 <= i + steps < count]


def exchange(parts, groups):
    return lax.all_to_all(parts, ("chain", "rows"), 0, 0, tiled=True, axis_index_groups=groups)


def local(video, cotangent, w_time, w_space):
    cot = cotangent[0]
    own = video[0].reshape(FRAMES * CELLS, CH_IN)
    rows, chain = lax.axis_size("rows"), lax.axis_size("chain")
    w_space = w_space.transpose(0, 1, 3, 2).reshape(9, CH_OUT, CH_IN)
    low = lax.ppermute(cot[:, 2 * BAND - 1 :], "rows", along("rows", 1))
    high = lax.ppermute(cot[:, :1], "rows", along("rows", -1))
    carried = lax.ppermute(own, "chain", along("chain", 1))
    operands = [pltpu.with_memory_space_constraint(value, pltpu.HBM) for value in (cot, own, w_time, w_space)]
    cot, own, w_time, w_space, inner, grad, hidden = inner_terms(*operands)
    grad_hidden, outer, returned = grad_terms(cot, low, high, w_space, w_time, grad)
    keep, send = block_terms(own, carried, w_time, inner, outer, grad_hidden, hidden)
    received = lax.ppermute(send, "clip", [(0, 1), (1, 0)])
    ours = video_terms(grad_hidden, w_time)
    received, ours = lax.optimization_barrier((received, ours))

    def device(c, x, z):
        return c * rows + x * N_Z + z

    near = [
        [device(2 * ch + c, x, 2 * zh + z) for x in range(N_X) for c in range(2) for z in range(2)]
        for ch in range(chain // 2)
        for zh in range(N_Z // 2)
    ]
    far = [
        [device(4 * c2 + 2 * c + c0, x, 2 * zh + zl) for c in range(2) for zh in range(N_Z // 2)]
        for c2 in range(chain // 4)
        for c0 in range(2)
        for x in range(N_X)
        for zl in range(2)
    ]
    share = pair_sum(keep.reshape(-1, LANES), received.reshape(-1, LANES))
    share = group_sum(exchange(share.reshape(4 * N_X, -1, LANES), near))
    share, returned = lax.optimization_barrier((share, returned))
    following = lax.ppermute(returned, "chain", along("chain", -1))
    share, following = lax.optimization_barrier((exchange(share.reshape(N_Z, PIECE, LANES), far), following))
    share = group_sum(share, 2 * chain)
    pieces = lax.all_to_all(share, ("chain", "clip"), 0, 0, tiled=True)
    voxels = 2 * chain * 2 * FRAMES * rows * 2 * BAND * 2 * COLS
    grad_time, grad_space, grad_video = unpack(pieces, ours, following, 1.0 / math.sqrt(voxels))
    return grad_video.reshape(video.shape), grad_time, grad_space.T


def solution(mesh):
    placed = P("clip", "chain", "rows", None, None)
    return jax.shard_map(
        local,
        mesh=mesh,
        in_specs=(placed, placed, P(), P()),
        out_specs=(placed, P("rows", None), P("rows", None)),
        check_vma=False,
    )
```

```python
import math

import jax
import jax.numpy as jnp
from jax import lax
from jax.experimental import pallas as pl
from jax.experimental.pallas import tpu as pltpu
from jax.sharding import PartitionSpec as P

FRAMES, BAND, COLS, CH_IN, CH_OUT = 2, 2, 48, 384, 192
CELLS = BAND * COLS
N_X, N_Z = 4, 8
F32, BF16 = jnp.float32, jnp.bfloat16
LANES = 128
PIECE, LINES = 48, 384
TIME_ROWS, SPACE_ROWS = 36, 108


def dot(a, b):
    return jnp.dot(a, b, preferred_element_type=F32)


def dot_rows(a, b):
    return lax.dot_general(a, b, (((1,), (1,)), ((), ())), preferred_element_type=F32)


def dot_t(a, b):
    return lax.dot_general(a, b, (((0,), (0,)), ((), ())), preferred_element_type=F32)


VMEM = pl.BlockSpec(memory_space=pltpu.VMEM)


def params(mib):
    return pltpu.CompilerParams(vmem_limit_bytes=mib * 1024 * 1024)


def picker():
    row = lax.broadcasted_iota(jnp.int32, (3 * COLS, 2 * COLS), 0)
    col = lax.broadcasted_iota(jnp.int32, (3 * COLS, 2 * COLS), 1)
    first = 2 * (row % COLS) + 1 - row // COLS
    return jnp.where((col == first) | (col == first + 1), 1.0, 0.0).astype(BF16)


HALF = 2 * FRAMES * COLS


def put(z, row, s, both):
    for c in range(3):
        z[row + c, s * COLS : (s + 1) * COLS] = both[c * COLS : (c + 1) * COLS]


INNER, OUTER = ((0, 1), (1, 1), (0, 0), (1, 2)), ((0, 2), (1, 0))


def taps(z, which, w_space):
    sums = [0.0, 0.0]
    for i, (p, a) in enumerate(which):
        for c in range(3):
            sums[p] = sums[p] + dot(z[3 * i + c], w_space[3 * a + c])
    return sums


def inner_kernel(cot_in, video_in, w_time_in, w_space_in, cot, video, w_time, w_space, inner, grad, hidden, sems):
    copies = [
        pltpu.make_async_copy(source, target, sems.at[i])
        for i, (source, target) in enumerate(
            ((cot_in, cot), (w_space_in, w_space), (video_in, video), (w_time_in, w_time))
        )
    ]
    for copy in copies:
        copy.start()
    pick = picker()
    copies[0].wait()
    for s in range(2 * FRAMES):
        reach = [dot(pick, cot[s, p]) for p in range(2 * BAND)]
        for i, (p, a) in enumerate(INNER):
            put(inner, 3 * i, s, (reach[2 * p + 1 - a] + reach[2 * p + 2 - a]).astype(BF16))
    copies[1].wait()
    grad[...] = jnp.concatenate(taps(inner, INNER, w_space))
    copies[2].wait()
    copies[3].wait()
    hidden[:CELLS] = dot(video[:CELLS], w_time[2])
    hidden[CELLS:] = dot(video[:CELLS], w_time[1]) + dot(video[CELLS:], w_time[2])


def inner_terms(cot, video, w_time, w_space):
    cells = FRAMES * CELLS
    return pl.pallas_call(
        inner_kernel,
        name="inner_terms",
        out_shape=(
            *(jax.ShapeDtypeStruct(array.shape, BF16) for array in (cot, video, w_time, w_space)),
            jax.ShapeDtypeStruct((3 * len(INNER), HALF, CH_OUT), BF16),
            jax.ShapeDtypeStruct((2 * cells, CH_IN), F32),
            jax.ShapeDtypeStruct((cells, 2 * CH_IN), F32),
        ),
        in_specs=[pl.BlockSpec(memory_space=pltpu.HBM)] * 4,
        out_specs=(VMEM,) * 7,
        scratch_shapes=[pltpu.SemaphoreType.DMA((4,))],
        compiler_params=params(16),
        cost_estimate=pl.CostEstimate(flops=1_500_000_000, bytes_accessed=6_000_000, transcendentals=0),
    )(cot, video, w_time, w_space)


def grad_kernel(cot, low, high, w_space, grad_in, grad_hidden, outer):
    pick = picker()
    for s in range(2 * FRAMES):
        put(outer, 0, s, (dot(pick, low[s, 0]) + dot(pick, cot[s, 0])).astype(BF16))
        put(outer, 3, s, (dot(pick, cot[s, 2 * BAND - 1]) + dot(pick, high[s, 0])).astype(BF16))
    for p, part in enumerate(taps(outer, OUTER, w_space)):
        part = part + grad_in[p * HALF : (p + 1) * HALF]
        for t in range(FRAMES):
            for j in range(2):
                s = 2 * t + j
                grad_hidden[(t * BAND + p) * COLS : (t * BAND + p + 1) * COLS, j * CH_IN : (j + 1) * CH_IN] = part[
                    s * COLS : (s + 1) * COLS
                ].astype(BF16)


def grad_terms(cot, low, high, w_space, grad):
    return pl.pallas_call(
        grad_kernel,
        name="grad_terms",
        out_shape=(
            jax.ShapeDtypeStruct((FRAMES * CELLS, 2 * CH_IN), BF16),
            jax.ShapeDtypeStruct((3 * len(OUTER), HALF, CH_OUT), BF16),
        ),
        in_specs=[VMEM] * 5,
        out_specs=(VMEM,) * 2,
        compiler_params=params(8),
        cost_estimate=pl.CostEstimate(flops=800_000_000, bytes_accessed=4_000_000, transcendentals=0),
    )(cot, low, high, w_space, grad)


def block_kernel(
    video, carried, w_time, inner, outer, grad_hidden, hidden_in,
    keep, send,
    ext, hid, time_acc, space_acc,
):
    ext[0 : FRAMES * CELLS] = carried[...]
    ext[FRAMES * CELLS :] = video[...]
    first = hidden_in[:CELLS] + dot(carried[:CELLS], w_time[0]) + dot(carried[CELLS:], w_time[1])
    second = hidden_in[CELLS:] + dot(carried[CELLS:], w_time[0])
    for t, hidden in enumerate((first, second)):
        for p in range(BAND):
            for j in range(2):
                start = (p * 2 * FRAMES + 2 * t + j) * COLS
                hid[start : start + COLS] = hidden[
                    p * COLS : (p + 1) * COLS, j * CH_IN : (j + 1) * CH_IN
                ].astype(BF16)

    for k in range(3):
        time_acc[k * CH_IN : (k + 1) * CH_IN] = dot_t(ext[k * CELLS : (k + FRAMES) * CELLS], grad_hidden[...])
    hid_t = [hid[p * HALF : (p + 1) * HALF].T for p in range(BAND)]
    where = {key: (z, 3 * i) for z, order in ((inner, INNER), (outer, OUTER)) for i, key in enumerate(order)}
    for a in range(3):
        for c in range(3):
            total = 0.0
            for p in range(BAND):
                z, row = where[p, a]
                total = total + dot(hid_t[p], z[row + c])
            tap = 3 * a + c
            space_acc[tap * CH_IN : (tap + 1) * CH_IN] = total

    mine = lax.axis_index("clip") == 0
    half = SPACE_ROWS // 2
    for r in range(N_X * N_Z):
        x, zh, zl = r // N_Z, r % N_Z // 2, r % 2
        t0, s0 = r * TIME_ROWS, r * SPACE_ROWS
        lines = [time_acc[t0 : t0 + TIME_ROWS, j * LANES : (j + 1) * LANES] for j in range(6)]
        lines.append(space_acc[s0 : s0 + SPACE_ROWS, 0:LANES])
        rest = [space_acc[s0 + i * half : s0 + (i + 1) * half, LANES:CH_OUT] for i in range(2)]
        lines.append(jnp.concatenate(rest, axis=1))
        lines.append(jnp.zeros((6, LANES), F32))
        lines = jnp.concatenate(lines, axis=0).astype(BF16)
        upper, lower = lines[: LINES // 2], lines[LINES // 2 :]
        mine_half, other_half = jnp.where(mine, upper, lower), jnp.where(mine, lower, upper)
        for c0 in range(2):
            for c1 in range(2):
                piece = (c0 * 2 + c1) * PIECE
                keep[x, zl, c0, c1, zh] = mine_half[piece : piece + PIECE]
                send[x, zl, c0, c1, zh] = other_half[piece : piece + PIECE]


def block_terms(video, carried, w_time, inner, outer, grad_hidden, hidden):
    cells = FRAMES * CELLS
    half = jax.ShapeDtypeStruct((N_X, 2, 2, 2, N_Z // 2, PIECE, LANES), BF16)
    return pl.pallas_call(
        block_kernel,
        name="block_terms",
        out_shape=(half, half),
        in_specs=[VMEM] * 7,
        out_specs=(VMEM,) * 2,
        scratch_shapes=[
            pltpu.VMEM((2 * cells, CH_IN), BF16),
            pltpu.VMEM((2 * cells, CH_IN), BF16),
            pltpu.VMEM((3 * CH_IN, 2 * CH_IN), F32),
            pltpu.VMEM((9 * CH_IN, CH_OUT), F32),
        ],
        compiler_params=params(20),
        cost_estimate=pl.CostEstimate(flops=3_000_000_000, bytes_accessed=12_000_000, transcendentals=0),
    )(video, carried, w_time, inner, outer, grad_hidden, hidden)


def pair_kernel(a, b, out):
    out[...] = (a[...].astype(F32) + b[...].astype(F32)).astype(BF16)


def pair_sum(a, b):
    return pl.pallas_call(
        pair_kernel,
        name="pair_sum",
        out_shape=jax.ShapeDtypeStruct(a.shape, BF16),
        in_specs=[VMEM] * 2,
        out_specs=VMEM,
        compiler_params=params(8),
    )(a, b)


def group_kernel(copies, parts, out):
    total = parts[0].astype(F32)
    for i in range(1, parts.shape[0]):
        total = total + parts[i].astype(F32)
    total = total.astype(BF16)
    if copies is None:
        out[...] = total
    else:
        for i in range(copies):
            out[i] = total


def group_sum(parts, copies=None):
    lead = () if copies is None else (copies,)
    return pl.pallas_call(
        lambda *refs: group_kernel(copies, *refs),
        name="group_sum",
        out_shape=jax.ShapeDtypeStruct(lead + parts.shape[1:], BF16),
        in_specs=[VMEM],
        out_specs=VMEM,
        compiler_params=params(8),
    )(parts)


def unpack_kernel(scale, pieces, own, following, time, space, video, line):
    video[...] = (own[...] + following[...].astype(F32)).astype(BF16)
    for k in range(2):
        for c0 in range(2):
            for c1 in range(2):
                low = (c1 * 2 + c0) * 2 + k
                start = ((k * 2 + c0) * 2 + c1) * PIECE
                total = pieces[low].astype(F32) + pieces[8 + low].astype(F32)
                line[start : start + PIECE] = total * scale
    for j in range(6):
        time[:, j * LANES : (j + 1) * LANES] = line[j * TIME_ROWS : (j + 1) * TIME_ROWS].astype(BF16)
    space[0:LANES] = line[216 : 216 + LANES].T[:, :SPACE_ROWS].astype(BF16)
    half = SPACE_ROWS // 2
    rest = line[324 : 324 + 64].T
    space[LANES:] = jnp.concatenate([rest[0:64, :half], rest[64:, :half]], axis=1).astype(BF16)


def unpack(pieces, own, following, scale):
    return pl.pallas_call(
        lambda *refs: unpack_kernel(scale, *refs),
        name="unpack",
        out_shape=(
            jax.ShapeDtypeStruct((TIME_ROWS, 6 * LANES), BF16),
            jax.ShapeDtypeStruct((CH_OUT, SPACE_ROWS), BF16),
            jax.ShapeDtypeStruct(own.shape, BF16),
        ),
        in_specs=[VMEM] * 3,
        out_specs=(VMEM,) * 3,
        scratch_shapes=[pltpu.VMEM((LINES + 8, LANES), F32)],
        compiler_params=params(8),
    )(pieces, own, following)


def video_kernel(grad_hidden, w_time, ours, returned):
    first, second = grad_hidden[:CELLS], grad_hidden[CELLS:]
    ours[:CELLS] = dot_rows(first, w_time[2]) + dot_rows(second, w_time[1])
    ours[CELLS:] = dot_rows(second, w_time[2])
    returned[:CELLS] = dot_rows(first, w_time[0]).astype(BF16)
    returned[CELLS:] = (dot_rows(first, w_time[1]) + dot_rows(second, w_time[0])).astype(BF16)


def video_terms(grad_hidden, w_time):
    return pl.pallas_call(
        video_kernel,
        name="video_terms",
        out_shape=(
            jax.ShapeDtypeStruct((FRAMES * CELLS, CH_IN), F32),
            jax.ShapeDtypeStruct((FRAMES * CELLS, CH_IN), BF16),
        ),
        in_specs=[VMEM] * 2,
        out_specs=(VMEM,) * 2,
        compiler_params=params(8),
        cost_estimate=pl.CostEstimate(flops=700_000_000, bytes_accessed=2_500_000, transcendentals=0),
    )(grad_hidden, w_time)


def along(axis, steps):
    count = lax.axis_size(axis)
    return [(i, i + steps) for i in range(count) if 0 <= i + steps < count]


def exchange(parts, groups):
    return lax.all_to_all(parts, ("chain", "rows"), 0, 0, tiled=True, axis_index_groups=groups)


def local(video, cotangent, w_time, w_space):
    cot = cotangent[0]
    own = video[0].reshape(FRAMES * CELLS, CH_IN)
    rows, chain = lax.axis_size("rows"), lax.axis_size("chain")
    w_space = w_space.transpose(0, 1, 3, 2).reshape(9, CH_OUT, CH_IN)
    low = lax.ppermute(cot[:, 2 * BAND - 1 :], "rows", along("rows", 1))
    high = lax.ppermute(cot[:, :1], "rows", along("rows", -1))
    carried = lax.ppermute(own, "chain", along("chain", 1))
    operands = [pltpu.with_memory_space_constraint(value, pltpu.HBM) for value in (cot, own, w_time, w_space)]
    cot, own, w_time, w_space, inner, grad, hidden = inner_terms(*operands)
    grad_hidden, outer = grad_terms(cot, low, high, w_space, grad)
    keep, send = block_terms(own, carried, w_time, inner, outer, grad_hidden, hidden)
    received = lax.ppermute(send, "clip", [(0, 1), (1, 0)])
    ours, returned = video_terms(grad_hidden, w_time)
    received, ours = lax.optimization_barrier((received, ours))

    def device(c, x, z):
        return c * rows + x * N_Z + z

    near = [
        [device(2 * ch + c, x, 2 * zh + z) for x in range(N_X) for z in range(2) for c in range(2)]
        for ch in range(chain // 2)
        for zh in range(N_Z // 2)
    ]
    far = [
        [device(4 * c2 + 2 * c + c0, x, 2 * zh + zl) for c in range(2) for zh in range(N_Z // 2)]
        for c2 in range(chain // 4)
        for c0 in range(2)
        for x in range(N_X)
        for zl in range(2)
    ]
    share = pair_sum(keep.reshape(-1, LANES), received.reshape(-1, LANES))
    share = group_sum(exchange(share.reshape(4 * N_X, -1, LANES), near))
    share, returned = lax.optimization_barrier((share, returned))
    following = lax.ppermute(returned, "chain", along("chain", -1))
    share, following = lax.optimization_barrier((exchange(share.reshape(N_Z, PIECE, LANES), far), following))
    share = group_sum(share, 2 * chain)
    pieces = lax.all_to_all(share, ("chain", "clip"), 0, 0, tiled=True)
    voxels = 2 * chain * 2 * FRAMES * rows * 2 * BAND * 2 * COLS
    grad_time, grad_space, grad_video = unpack(pieces, ours, following, 1.0 / math.sqrt(voxels))
    return grad_video.reshape(video.shape), grad_time, grad_space.T


def solution(mesh):
    placed = P("clip", "chain", "rows", None, None)
    return jax.shard_map(
        local,
        mesh=mesh,
        in_specs=(placed, placed, P(), P()),
        out_specs=(placed, P("rows", None), P("rows", None)),
        check_vma=False,
    )
```

```python
import math

import jax
import jax.numpy as jnp
from jax import lax
from jax.experimental import pallas as pl
from jax.experimental.pallas import tpu as pltpu
from jax.sharding import PartitionSpec as P

FRAMES, BAND, COLS, CH_IN, CH_OUT = 2, 2, 48, 384, 192
CELLS = BAND * COLS
N_X, N_Z = 4, 8
F32, BF16 = jnp.float32, jnp.bfloat16
LANES = 128
PIECE, LINES = 48, 384
TIME_ROWS, SPACE_ROWS = 36, 108


def dot(a, b):
    return jnp.dot(a, b, preferred_element_type=F32)


def dot_rows(a, b):
    return lax.dot_general(a, b, (((1,), (1,)), ((), ())), preferred_element_type=F32)


def dot_t(a, b):
    return lax.dot_general(a, b, (((0,), (0,)), ((), ())), preferred_element_type=F32)


VMEM = pl.BlockSpec(memory_space=pltpu.VMEM)


def params(mib):
    return pltpu.CompilerParams(vmem_limit_bytes=mib * 1024 * 1024)


def picker():
    row = lax.broadcasted_iota(jnp.int32, (3 * COLS, 2 * COLS), 0)
    col = lax.broadcasted_iota(jnp.int32, (3 * COLS, 2 * COLS), 1)
    first = 2 * (row % COLS) + 1 - row // COLS
    return jnp.where((col == first) | (col == first + 1), 1.0, 0.0).astype(BF16)


HALF = 2 * FRAMES * COLS


def put(z, row, s, both):
    for c in range(3):
        z[row + c, s * COLS : (s + 1) * COLS] = both[c * COLS : (c + 1) * COLS]


INNER, OUTER = ((0, 1), (1, 1), (0, 0), (1, 2)), ((0, 2), (1, 0))


def taps(z, which, w_space):
    sums = [0.0, 0.0]
    for i, (p, a) in enumerate(which):
        for c in range(3):
            sums[p] = sums[p] + dot(z[3 * i + c], w_space[3 * a + c])
    return sums


def inner_kernel(cot_in, video_in, w_time_in, w_space_in, cot, video, w_time, w_space, inner, grad, hidden, sems):
    copies = [
        pltpu.make_async_copy(source, target, sems.at[i])
        for i, (source, target) in enumerate(
            ((cot_in, cot), (w_space_in, w_space), (video_in, video), (w_time_in, w_time))
        )
    ]
    for copy in copies:
        copy.start()
    pick = picker()
    copies[0].wait()
    for s in range(2 * FRAMES):
        reach = [dot(pick, cot[s, p]) for p in range(2 * BAND)]
        for i, (p, a) in enumerate(INNER):
            put(inner, 3 * i, s, (reach[2 * p + 1 - a] + reach[2 * p + 2 - a]).astype(BF16))
    copies[1].wait()
    grad[...] = jnp.concatenate(taps(inner, INNER, w_space))
    copies[2].wait()
    copies[3].wait()
    hidden[:CELLS] = dot(video[:CELLS], w_time[2])
    hidden[CELLS:] = dot(video[:CELLS], w_time[1]) + dot(video[CELLS:], w_time[2])


def inner_terms(cot, video, w_time, w_space):
    cells = FRAMES * CELLS
    return pl.pallas_call(
        inner_kernel,
        name="inner_terms",
        out_shape=(
            *(jax.ShapeDtypeStruct(array.shape, BF16) for array in (cot, video, w_time, w_space)),
            jax.ShapeDtypeStruct((3 * len(INNER), HALF, CH_OUT), BF16),
            jax.ShapeDtypeStruct((2 * cells, CH_IN), F32),
            jax.ShapeDtypeStruct((cells, 2 * CH_IN), F32),
        ),
        in_specs=[pl.BlockSpec(memory_space=pltpu.HBM)] * 4,
        out_specs=(VMEM,) * 7,
        scratch_shapes=[pltpu.SemaphoreType.DMA((4,))],
        compiler_params=params(16),
        cost_estimate=pl.CostEstimate(flops=1_500_000_000, bytes_accessed=6_000_000, transcendentals=0),
    )(cot, video, w_time, w_space)


def grad_kernel(cot, low, high, w_space, grad_in, grad_hidden, outer):
    pick = picker()
    for s in range(2 * FRAMES):
        put(outer, 0, s, (dot(pick, low[s, 0]) + dot(pick, cot[s, 0])).astype(BF16))
        put(outer, 3, s, (dot(pick, cot[s, 2 * BAND - 1]) + dot(pick, high[s, 0])).astype(BF16))
    for p, part in enumerate(taps(outer, OUTER, w_space)):
        part = part + grad_in[p * HALF : (p + 1) * HALF]
        for t in range(FRAMES):
            for j in range(2):
                s = 2 * t + j
                grad_hidden[(t * BAND + p) * COLS : (t * BAND + p + 1) * COLS, j * CH_IN : (j + 1) * CH_IN] = part[
                    s * COLS : (s + 1) * COLS
                ].astype(BF16)


def grad_terms(cot, low, high, w_space, grad):
    return pl.pallas_call(
        grad_kernel,
        name="grad_terms",
        out_shape=(
            jax.ShapeDtypeStruct((FRAMES * CELLS, 2 * CH_IN), BF16),
            jax.ShapeDtypeStruct((3 * len(OUTER), HALF, CH_OUT), BF16),
        ),
        in_specs=[VMEM] * 5,
        out_specs=(VMEM,) * 2,
        compiler_params=params(8),
        cost_estimate=pl.CostEstimate(flops=800_000_000, bytes_accessed=4_000_000, transcendentals=0),
    )(cot, low, high, w_space, grad)


def block_kernel(
    video, carried, w_time, inner, outer, grad_hidden, hidden_in,
    keep, send,
    ext, hid, time_acc, space_acc,
):
    ext[0 : FRAMES * CELLS] = carried[...]
    ext[FRAMES * CELLS :] = video[...]
    first = hidden_in[:CELLS] + dot(carried[:CELLS], w_time[0]) + dot(carried[CELLS:], w_time[1])
    second = hidden_in[CELLS:] + dot(carried[CELLS:], w_time[0])
    for t, hidden in enumerate((first, second)):
        for p in range(BAND):
            for j in range(2):
                start = (p * 2 * FRAMES + 2 * t + j) * COLS
                hid[start : start + COLS] = hidden[
                    p * COLS : (p + 1) * COLS, j * CH_IN : (j + 1) * CH_IN
                ].astype(BF16)

    for k in range(3):
        time_acc[k * CH_IN : (k + 1) * CH_IN] = dot_t(ext[k * CELLS : (k + FRAMES) * CELLS], grad_hidden[...])
    hid_t = [hid[p * HALF : (p + 1) * HALF].T for p in range(BAND)]
    where = {key: (z, 3 * i) for z, order in ((inner, INNER), (outer, OUTER)) for i, key in enumerate(order)}
    for a in range(3):
        for c in range(3):
            total = 0.0
            for p in range(BAND):
                z, row = where[p, a]
                total = total + dot(hid_t[p], z[row + c])
            tap = 3 * a + c
            space_acc[tap * CH_IN : (tap + 1) * CH_IN] = total

    mine = lax.axis_index("clip") == 0
    half = SPACE_ROWS // 2
    for r in range(N_X * N_Z):
        xh, xl, zh, zl = r // N_Z // 2, r // N_Z % 2, r % N_Z // 2, r % 2
        t0, s0 = r * TIME_ROWS, r * SPACE_ROWS
        lines = [time_acc[t0 : t0 + TIME_ROWS, j * LANES : (j + 1) * LANES] for j in range(6)]
        lines.append(space_acc[s0 : s0 + SPACE_ROWS, 0:LANES])
        rest = [space_acc[s0 + i * half : s0 + (i + 1) * half, LANES:CH_OUT] for i in range(2)]
        lines.append(jnp.concatenate(rest, axis=1))
        lines.append(jnp.zeros((6, LANES), F32))
        lines = jnp.concatenate(lines, axis=0).astype(BF16)
        upper, lower = lines[: LINES // 2], lines[LINES // 2 :]
        mine_half, other_half = jnp.where(mine, upper, lower), jnp.where(mine, lower, upper)
        for c0 in range(2):
            for c1 in range(2):
                piece = (c0 * 2 + c1) * PIECE
                keep[xl, zl, c0, xh, c1, zh] = mine_half[piece : piece + PIECE]
                send[xl, zl, c0, xh, c1, zh] = other_half[piece : piece + PIECE]


def block_terms(video, carried, w_time, inner, outer, grad_hidden, hidden):
    cells = FRAMES * CELLS
    half = jax.ShapeDtypeStruct((2, 2, 2, N_X // 2, 2, N_Z // 2, PIECE, LANES), BF16)
    return pl.pallas_call(
        block_kernel,
        name="block_terms",
        out_shape=(half, half),
        in_specs=[VMEM] * 7,
        out_specs=(VMEM,) * 2,
        scratch_shapes=[
            pltpu.VMEM((2 * cells, CH_IN), BF16),
            pltpu.VMEM((2 * cells, CH_IN), BF16),
            pltpu.VMEM((3 * CH_IN, 2 * CH_IN), F32),
            pltpu.VMEM((9 * CH_IN, CH_OUT), F32),
        ],
        compiler_params=params(20),
        cost_estimate=pl.CostEstimate(flops=3_000_000_000, bytes_accessed=12_000_000, transcendentals=0),
    )(video, carried, w_time, inner, outer, grad_hidden, hidden)


def pair_kernel(a, b, out):
    out[...] = (a[...].astype(F32) + b[...].astype(F32)).astype(BF16)


def pair_sum(a, b):
    return pl.pallas_call(
        pair_kernel,
        name="pair_sum",
        out_shape=jax.ShapeDtypeStruct(a.shape, BF16),
        in_specs=[VMEM] * 2,
        out_specs=VMEM,
        compiler_params=params(8),
    )(a, b)


def group_kernel(copies, parts, out):
    total = parts[0].astype(F32)
    for i in range(1, parts.shape[0]):
        total = total + parts[i].astype(F32)
    total = total.astype(BF16)
    if copies is None:
        out[...] = total
    else:
        for i in range(copies):
            out[i] = total


def group_sum(parts, copies=None):
    lead = () if copies is None else (copies,)
    return pl.pallas_call(
        lambda *refs: group_kernel(copies, *refs),
        name="group_sum",
        out_shape=jax.ShapeDtypeStruct(lead + parts.shape[1:], BF16),
        in_specs=[VMEM],
        out_specs=VMEM,
        compiler_params=params(8),
    )(parts)


def unpack_kernel(scale, pieces, own, following, time, space, video, line):
    video[...] = (own[...] + following[...].astype(F32)).astype(BF16)
    for k in range(2):
        for c0 in range(2):
            for c1 in range(2):
                low = (c1 * 2 + c0) * 2 + k
                start = ((k * 2 + c0) * 2 + c1) * PIECE
                total = pieces[low].astype(F32) + pieces[8 + low].astype(F32)
                line[start : start + PIECE] = total * scale
    for j in range(6):
        time[:, j * LANES : (j + 1) * LANES] = line[j * TIME_ROWS : (j + 1) * TIME_ROWS].astype(BF16)
    space[0:LANES] = line[216 : 216 + LANES].T[:, :SPACE_ROWS].astype(BF16)
    half = SPACE_ROWS // 2
    rest = line[324 : 324 + 64].T
    space[LANES:] = jnp.concatenate([rest[0:64, :half], rest[64:, :half]], axis=1).astype(BF16)


def unpack(pieces, own, following, scale):
    return pl.pallas_call(
        lambda *refs: unpack_kernel(scale, *refs),
        name="unpack",
        out_shape=(
            jax.ShapeDtypeStruct((TIME_ROWS, 6 * LANES), BF16),
            jax.ShapeDtypeStruct((CH_OUT, SPACE_ROWS), BF16),
            jax.ShapeDtypeStruct(own.shape, BF16),
        ),
        in_specs=[VMEM] * 3,
        out_specs=(VMEM,) * 3,
        scratch_shapes=[pltpu.VMEM((LINES + 8, LANES), F32)],
        compiler_params=params(8),
    )(pieces, own, following)


def video_kernel(grad_hidden, w_time, ours, returned):
    first, second = grad_hidden[:CELLS], grad_hidden[CELLS:]
    ours[:CELLS] = dot_rows(first, w_time[2]) + dot_rows(second, w_time[1])
    ours[CELLS:] = dot_rows(second, w_time[2])
    returned[:CELLS] = dot_rows(first, w_time[0]).astype(BF16)
    returned[CELLS:] = (dot_rows(first, w_time[1]) + dot_rows(second, w_time[0])).astype(BF16)


def video_terms(grad_hidden, w_time):
    return pl.pallas_call(
        video_kernel,
        name="video_terms",
        out_shape=(
            jax.ShapeDtypeStruct((FRAMES * CELLS, CH_IN), F32),
            jax.ShapeDtypeStruct((FRAMES * CELLS, CH_IN), BF16),
        ),
        in_specs=[VMEM] * 2,
        out_specs=(VMEM,) * 2,
        compiler_params=params(8),
        cost_estimate=pl.CostEstimate(flops=700_000_000, bytes_accessed=2_500_000, transcendentals=0),
    )(grad_hidden, w_time)


def along(axis, steps):
    count = lax.axis_size(axis)
    return [(i, i + steps) for i in range(count) if 0 <= i + steps < count]


def exchange(parts, axes, groups=None):
    return lax.all_to_all(parts, axes, 0, 0, tiled=True, axis_index_groups=groups)


def local(video, cotangent, w_time, w_space):
    cot = cotangent[0]
    own = video[0].reshape(FRAMES * CELLS, CH_IN)
    rows, chain = lax.axis_size("rows"), lax.axis_size("chain")
    w_space = w_space.transpose(0, 1, 3, 2).reshape(9, CH_OUT, CH_IN)
    low = lax.ppermute(cot[:, 2 * BAND - 1 :], "rows", along("rows", 1))
    high = lax.ppermute(cot[:, :1], "rows", along("rows", -1))
    carried = lax.ppermute(own, "chain", along("chain", 1))
    operands = [pltpu.with_memory_space_constraint(value, pltpu.HBM) for value in (cot, own, w_time, w_space)]
    cot, own, w_time, w_space, inner, grad, hidden = inner_terms(*operands)
    grad_hidden, outer = grad_terms(cot, low, high, w_space, grad)
    keep, send = block_terms(own, carried, w_time, inner, outer, grad_hidden, hidden)
    received = lax.ppermute(send, "clip", [(0, 1), (1, 0)])
    ours, returned = video_terms(grad_hidden, w_time)
    received, ours = lax.optimization_barrier((received, ours))

    def device(c, x, z):
        return c * rows + x * N_Z + z

    def pair(index, core, count):
        return sorted(((2 * index + core) % count, (2 * index + core + 1) % count), key=lambda i: i % 2)

    near = [
        [
            2 * device(c, x, z) + core
            for x in pair(xh, core, N_X)
            for z in pair(zh, core, N_Z)
            for c in pair(ch, core, chain)
        ]
        for core in range(2)
        for xh in range(N_X // 2)
        for ch in range(chain // 2)
        for zh in range(N_Z // 2)
    ]
    far = [
        [
            device(4 * c2 + 2 * c + c0, 2 * xh + xl, 2 * zh + zl)
            for xh in range(N_X // 2)
            for c in range(2)
            for zh in range(N_Z // 2)
        ]
        for c2 in range(chain // 4)
        for c0 in range(2)
        for xl in range(2)
        for zl in range(2)
    ]
    share = pair_sum(keep.reshape(-1, LANES), received.reshape(-1, LANES))
    share = group_sum(exchange(share.reshape(8, -1, LANES), ("chain", "rows", "clip"), near))
    share, returned = lax.optimization_barrier((share, returned))
    following = lax.ppermute(returned, "chain", along("chain", -1))
    share, following = lax.optimization_barrier((exchange(share.reshape(2 * N_Z, PIECE, LANES), ("chain", "rows"), far), following))
    share = group_sum(share, 2 * chain)
    pieces = exchange(share, ("chain", "clip"))
    voxels = 2 * chain * 2 * FRAMES * rows * 2 * BAND * 2 * COLS
    grad_time, grad_space, grad_video = unpack(pieces, ours, following, 1.0 / math.sqrt(voxels))
    return grad_video.reshape(video.shape), grad_time, grad_space.T


def solution(mesh):
    placed = P("clip", "chain", "rows", None, None)
    return jax.shard_map(
        local,
        mesh=mesh,
        in_specs=(placed, placed, P(), P()),
        out_specs=(placed, P("rows", None), P("rows", None)),
        check_vma=False,
    )
```

```python
import math

import jax
import jax.numpy as jnp
from jax import lax
from jax.experimental import pallas as pl
from jax.experimental.pallas import tpu as pltpu
from jax.sharding import PartitionSpec as P

FRAMES, BAND, COLS, CH_IN, CH_OUT = 2, 2, 48, 384, 192
CELLS = BAND * COLS
N_X, N_Z = 4, 8
F32, BF16 = jnp.float32, jnp.bfloat16
LANES = 128
PIECE, LINES = 48, 384
TIME_ROWS, SPACE_ROWS = 36, 108


def dot(a, b):
    return jnp.dot(a, b, preferred_element_type=F32)


def dot_rows(a, b):
    return lax.dot_general(a, b, (((1,), (1,)), ((), ())), preferred_element_type=F32)


def dot_t(a, b):
    return lax.dot_general(a, b, (((0,), (0,)), ((), ())), preferred_element_type=F32)


VMEM = pl.BlockSpec(memory_space=pltpu.VMEM)


def params(mib):
    return pltpu.CompilerParams(vmem_limit_bytes=mib * 1024 * 1024)


def picker():
    row = lax.broadcasted_iota(jnp.int32, (3 * COLS, 2 * COLS), 0)
    col = lax.broadcasted_iota(jnp.int32, (3 * COLS, 2 * COLS), 1)
    first = 2 * (row % COLS) + 1 - row // COLS
    return jnp.where((col == first) | (col == first + 1), 1.0, 0.0).astype(BF16)


HALF = 2 * FRAMES * COLS


def put(z, row, s, both):
    for c in range(3):
        z[row + c, s * COLS : (s + 1) * COLS] = both[c * COLS : (c + 1) * COLS]


INNER, OUTER = ((0, 1), (1, 1), (0, 0), (1, 2)), ((0, 2), (1, 0))


def taps(z, which, w_space):
    sums = [0.0, 0.0]
    for i, (p, a) in enumerate(which):
        for c in range(3):
            sums[p] = sums[p] + dot(z[3 * i + c], w_space[3 * a + c])
    return sums


def inner_kernel(cot_in, video_in, w_time_in, w_space_in, cot, video, w_time, w_space, inner, grad, hidden, sems):
    copies = [
        pltpu.make_async_copy(source, target, sems.at[i])
        for i, (source, target) in enumerate(
            ((cot_in, cot), (w_space_in, w_space), (video_in, video), (w_time_in, w_time))
        )
    ]
    for copy in copies:
        copy.start()
    pick = picker()
    copies[0].wait()
    for s in range(2 * FRAMES):
        reach = [dot(pick, cot[s, p]) for p in range(2 * BAND)]
        for i, (p, a) in enumerate(INNER):
            put(inner, 3 * i, s, (reach[2 * p + 1 - a] + reach[2 * p + 2 - a]).astype(BF16))
    copies[1].wait()
    grad[...] = jnp.concatenate(taps(inner, INNER, w_space))
    copies[2].wait()
    copies[3].wait()
    hidden[:CELLS] = dot(video[:CELLS], w_time[2])
    hidden[CELLS:] = dot(video[:CELLS], w_time[1]) + dot(video[CELLS:], w_time[2])


def inner_terms(cot, video, w_time, w_space):
    cells = FRAMES * CELLS
    return pl.pallas_call(
        inner_kernel,
        name="inner_terms",
        out_shape=(
            *(jax.ShapeDtypeStruct(array.shape, BF16) for array in (cot, video, w_time, w_space)),
            jax.ShapeDtypeStruct((3 * len(INNER), HALF, CH_OUT), BF16),
            jax.ShapeDtypeStruct((2 * cells, CH_IN), F32),
            jax.ShapeDtypeStruct((cells, 2 * CH_IN), F32),
        ),
        in_specs=[pl.BlockSpec(memory_space=pltpu.HBM)] * 4,
        out_specs=(VMEM,) * 7,
        scratch_shapes=[pltpu.SemaphoreType.DMA((4,))],
        compiler_params=params(16),
        cost_estimate=pl.CostEstimate(flops=1_500_000_000, bytes_accessed=6_000_000, transcendentals=0),
    )(cot, video, w_time, w_space)


def grad_kernel(cot, low, high, w_space, grad_in, grad_hidden, outer):
    pick = picker()
    for s in range(2 * FRAMES):
        put(outer, 0, s, (dot(pick, low[s, 0]) + dot(pick, cot[s, 0])).astype(BF16))
        put(outer, 3, s, (dot(pick, cot[s, 2 * BAND - 1]) + dot(pick, high[s, 0])).astype(BF16))
    for p, part in enumerate(taps(outer, OUTER, w_space)):
        part = part + grad_in[p * HALF : (p + 1) * HALF]
        for t in range(FRAMES):
            for j in range(2):
                s = 2 * t + j
                grad_hidden[(t * BAND + p) * COLS : (t * BAND + p + 1) * COLS, j * CH_IN : (j + 1) * CH_IN] = part[
                    s * COLS : (s + 1) * COLS
                ].astype(BF16)


def grad_terms(cot, low, high, w_space, grad):
    return pl.pallas_call(
        grad_kernel,
        name="grad_terms",
        out_shape=(
            jax.ShapeDtypeStruct((FRAMES * CELLS, 2 * CH_IN), BF16),
            jax.ShapeDtypeStruct((3 * len(OUTER), HALF, CH_OUT), BF16),
        ),
        in_specs=[VMEM] * 5,
        out_specs=(VMEM,) * 2,
        compiler_params=params(8),
        cost_estimate=pl.CostEstimate(flops=800_000_000, bytes_accessed=4_000_000, transcendentals=0),
    )(cot, low, high, w_space, grad)


def block_kernel(
    video, carried, w_time, inner, outer, grad_hidden, hidden_in,
    keep, send,
    ext, hid, time_acc, space_acc,
):
    ext[0 : FRAMES * CELLS] = carried[...]
    ext[FRAMES * CELLS :] = video[...]
    first = hidden_in[:CELLS] + dot(carried[:CELLS], w_time[0]) + dot(carried[CELLS:], w_time[1])
    second = hidden_in[CELLS:] + dot(carried[CELLS:], w_time[0])
    for t, hidden in enumerate((first, second)):
        for p in range(BAND):
            for j in range(2):
                start = (p * 2 * FRAMES + 2 * t + j) * COLS
                hid[start : start + COLS] = hidden[
                    p * COLS : (p + 1) * COLS, j * CH_IN : (j + 1) * CH_IN
                ].astype(BF16)

    for k in range(3):
        time_acc[k * CH_IN : (k + 1) * CH_IN] = dot_t(ext[k * CELLS : (k + FRAMES) * CELLS], grad_hidden[...])
    hid_t = [hid[p * HALF : (p + 1) * HALF].T for p in range(BAND)]
    where = {key: (z, 3 * i) for z, order in ((inner, INNER), (outer, OUTER)) for i, key in enumerate(order)}
    for a in range(3):
        for c in range(3):
            total = 0.0
            for p in range(BAND):
                z, row = where[p, a]
                total = total + dot(hid_t[p], z[row + c])
            tap = 3 * a + c
            space_acc[tap * CH_IN : (tap + 1) * CH_IN] = total

    mine = lax.axis_index("clip") == 0
    half = SPACE_ROWS // 2
    for r in range(N_X * N_Z):
        xh, xl, zh, zl = r // N_Z // 2, r // N_Z % 2, r % N_Z // 2, r % 2
        t0, s0 = r * TIME_ROWS, r * SPACE_ROWS
        lines = [time_acc[t0 : t0 + TIME_ROWS, j * LANES : (j + 1) * LANES] for j in range(6)]
        lines.append(space_acc[s0 : s0 + SPACE_ROWS, 0:LANES])
        rest = [space_acc[s0 + i * half : s0 + (i + 1) * half, LANES:CH_OUT] for i in range(2)]
        lines.append(jnp.concatenate(rest, axis=1))
        lines.append(jnp.zeros((6, LANES), F32))
        lines = jnp.concatenate(lines, axis=0).astype(BF16)
        upper, lower = lines[: LINES // 2], lines[LINES // 2 :]
        mine_half, other_half = jnp.where(mine, upper, lower), jnp.where(mine, lower, upper)
        for c0 in range(2):
            for c1 in range(2):
                piece = (c0 * 2 + c1) * PIECE
                keep[xl, zl, c0, xh, c1, zh] = mine_half[piece : piece + PIECE]
                send[xl, zl, c0, xh, c1, zh] = other_half[piece : piece + PIECE]


def block_terms(video, carried, w_time, inner, outer, grad_hidden, hidden):
    cells = FRAMES * CELLS
    half = jax.ShapeDtypeStruct((2, 2, 2, N_X // 2, 2, N_Z // 2, PIECE, LANES), BF16)
    return pl.pallas_call(
        block_kernel,
        name="block_terms",
        out_shape=(half, half),
        in_specs=[VMEM] * 7,
        out_specs=(VMEM,) * 2,
        scratch_shapes=[
            pltpu.VMEM((2 * cells, CH_IN), BF16),
            pltpu.VMEM((2 * cells, CH_IN), BF16),
            pltpu.VMEM((3 * CH_IN, 2 * CH_IN), F32),
            pltpu.VMEM((9 * CH_IN, CH_OUT), F32),
        ],
        compiler_params=params(20),
        cost_estimate=pl.CostEstimate(flops=3_000_000_000, bytes_accessed=12_000_000, transcendentals=0),
    )(video, carried, w_time, inner, outer, grad_hidden, hidden)


def pair_kernel(a, b, out):
    out[...] = (a[...].astype(F32) + b[...].astype(F32)).astype(BF16)


def pair_sum(a, b):
    return pl.pallas_call(
        pair_kernel,
        name="pair_sum",
        out_shape=jax.ShapeDtypeStruct(a.shape, BF16),
        in_specs=[VMEM] * 2,
        out_specs=VMEM,
        compiler_params=params(8),
    )(a, b)


def group_kernel(copies, parts, out):
    total = parts[0].astype(F32)
    for i in range(1, parts.shape[0]):
        total = total + parts[i].astype(F32)
    total = total.astype(BF16)
    if copies is None:
        out[...] = total
    else:
        for i in range(copies):
            out[i] = total


def group_sum(parts, copies=None):
    lead = () if copies is None else (copies,)
    return pl.pallas_call(
        lambda *refs: group_kernel(copies, *refs),
        name="group_sum",
        out_shape=jax.ShapeDtypeStruct(lead + parts.shape[1:], BF16),
        in_specs=[VMEM],
        out_specs=VMEM,
        compiler_params=params(8),
    )(parts)


def unpack_kernel(scale, pieces, own, following, time, space, video, line):
    video[...] = (own[...] + following[...].astype(F32)).astype(BF16)
    for k in range(2):
        for c0 in range(2):
            for c1 in range(2):
                low = (c1 * 2 + c0) * 2 + k
                start = ((k * 2 + c0) * 2 + c1) * PIECE
                total = pieces[low].astype(F32) + pieces[8 + low].astype(F32)
                line[start : start + PIECE] = total * scale
    for j in range(6):
        time[:, j * LANES : (j + 1) * LANES] = line[j * TIME_ROWS : (j + 1) * TIME_ROWS].astype(BF16)
    space[0:LANES] = line[216 : 216 + LANES].T[:, :SPACE_ROWS].astype(BF16)
    half = SPACE_ROWS // 2
    rest = line[324 : 324 + 64].T
    space[LANES:] = jnp.concatenate([rest[0:64, :half], rest[64:, :half]], axis=1).astype(BF16)


def unpack(pieces, own, following, scale):
    return pl.pallas_call(
        lambda *refs: unpack_kernel(scale, *refs),
        name="unpack",
        out_shape=(
            jax.ShapeDtypeStruct((TIME_ROWS, 6 * LANES), BF16),
            jax.ShapeDtypeStruct((CH_OUT, SPACE_ROWS), BF16),
            jax.ShapeDtypeStruct(own.shape, BF16),
        ),
        in_specs=[VMEM] * 3,
        out_specs=(VMEM,) * 3,
        scratch_shapes=[pltpu.VMEM((LINES + 8, LANES), F32)],
        compiler_params=params(8),
    )(pieces, own, following)


def video_kernel(grad_hidden, w_time, ours, returned):
    first, second = grad_hidden[:CELLS], grad_hidden[CELLS:]
    ours[:CELLS] = dot_rows(first, w_time[2]) + dot_rows(second, w_time[1])
    ours[CELLS:] = dot_rows(second, w_time[2])
    returned[:CELLS] = dot_rows(first, w_time[0]).astype(BF16)
    returned[CELLS:] = (dot_rows(first, w_time[1]) + dot_rows(second, w_time[0])).astype(BF16)


def video_terms(grad_hidden, w_time):
    return pl.pallas_call(
        video_kernel,
        name="video_terms",
        out_shape=(
            jax.ShapeDtypeStruct((FRAMES * CELLS, CH_IN), F32),
            jax.ShapeDtypeStruct((FRAMES * CELLS, CH_IN), BF16),
        ),
        in_specs=[VMEM] * 2,
        out_specs=(VMEM,) * 2,
        compiler_params=params(8),
        cost_estimate=pl.CostEstimate(flops=700_000_000, bytes_accessed=2_500_000, transcendentals=0),
    )(grad_hidden, w_time)


def along(axis, steps):
    count = lax.axis_size(axis)
    return [(i, i + steps) for i in range(count) if 0 <= i + steps < count]


def exchange(parts, axes, groups=None):
    return lax.all_to_all(parts, axes, 0, 0, tiled=True, axis_index_groups=groups)


def local(video, cotangent, w_time, w_space):
    cot = cotangent[0]
    own = video[0].reshape(FRAMES * CELLS, CH_IN)
    rows, chain = lax.axis_size("rows"), lax.axis_size("chain")
    w_space = w_space.transpose(0, 1, 3, 2).reshape(9, CH_OUT, CH_IN)
    low = lax.ppermute(cot[:, 2 * BAND - 1 :], "rows", along("rows", 1))
    high = lax.ppermute(cot[:, :1], "rows", along("rows", -1))
    carried = lax.ppermute(own, "chain", along("chain", 1))
    operands = [pltpu.with_memory_space_constraint(value, pltpu.HBM) for value in (cot, own, w_time, w_space)]
    cot, own, w_time, w_space, inner, grad, hidden = inner_terms(*operands)
    grad_hidden, outer = grad_terms(cot, low, high, w_space, grad)
    keep, send = block_terms(own, carried, w_time, inner, outer, grad_hidden, hidden)
    received = lax.ppermute(send, "clip", [(0, 1), (1, 0)])
    ours, returned = video_terms(grad_hidden, w_time)
    received, ours = lax.optimization_barrier((received, ours))

    def device(c, x, z):
        return c * rows + x * N_Z + z

    def pair(index, core, count):
        return sorted(((2 * index + core) % count, (2 * index + core + 1) % count), key=lambda i: i % 2)

    near = [
        [
            2 * device(c, x, z) + core
            for x in pair(xh, core, N_X)
            for z in pair(zh, core, N_Z)
            for c in pair(ch, core, chain)
        ]
        for core in range(2)
        for xh in range(N_X // 2)
        for ch in range(chain // 2)
        for zh in range(N_Z // 2)
    ]
    far = [
        [
            device(4 * c2 + 2 * c + c0, 2 * xh + xl, 2 * zh + zl)
            for xh in range(N_X // 2)
            for c in range(2)
            for zh in range(N_Z // 2)
        ]
        for c2 in range(chain // 4)
        for c0 in range(2)
        for xl in range(2)
        for zl in range(2)
    ]
    share = pair_sum(keep.reshape(-1, LANES), received.reshape(-1, LANES))
    share = group_sum(exchange(share.reshape(8, -1, LANES), ("chain", "rows", "clip"), near))
    share = group_sum(exchange(share.reshape(2 * N_Z, PIECE, LANES), ("chain", "rows"), far), 2 * chain)
    share, returned = lax.optimization_barrier((share, returned))
    following = lax.ppermute(returned, "chain", along("chain", -1))
    pieces = exchange(share, ("chain", "clip"))
    voxels = 2 * chain * 2 * FRAMES * rows * 2 * BAND * 2 * COLS
    grad_time, grad_space, grad_video = unpack(pieces, ours, following, 1.0 / math.sqrt(voxels))
    return grad_video.reshape(video.shape), grad_time, grad_space.T


def solution(mesh):
    placed = P("clip", "chain", "rows", None, None)
    return jax.shard_map(
        local,
        mesh=mesh,
        in_specs=(placed, placed, P(), P()),
        out_specs=(placed, P("rows", None), P("rows", None)),
        check_vma=False,
    )
```

```python
import math

import jax
import jax.numpy as jnp
from jax import lax
from jax.experimental import pallas as pl
from jax.experimental.pallas import tpu as pltpu
from jax.sharding import PartitionSpec as P

FRAMES, BAND, COLS, CH_IN, CH_OUT = 2, 2, 48, 384, 192
CELLS = BAND * COLS
N_X, N_Z = 4, 8
F32, BF16 = jnp.float32, jnp.bfloat16
LANES = 128
PIECE, LINES = 48, 384
TIME_ROWS, SPACE_ROWS = 36, 108


def dot(a, b):
    return jnp.dot(a, b, preferred_element_type=F32)


def dot_rows(a, b):
    return lax.dot_general(a, b, (((1,), (1,)), ((), ())), preferred_element_type=F32)


def dot_t(a, b):
    return lax.dot_general(a, b, (((0,), (0,)), ((), ())), preferred_element_type=F32)


VMEM = pl.BlockSpec(memory_space=pltpu.VMEM)


def params(mib):
    return pltpu.CompilerParams(vmem_limit_bytes=mib * 1024 * 1024)


def picker():
    row = lax.broadcasted_iota(jnp.int32, (3 * COLS, 2 * COLS), 0)
    col = lax.broadcasted_iota(jnp.int32, (3 * COLS, 2 * COLS), 1)
    first = 2 * (row % COLS) + 1 - row // COLS
    return jnp.where((col == first) | (col == first + 1), 1.0, 0.0).astype(BF16)


HALF = 2 * FRAMES * COLS


def put(z, row, s, both):
    for c in range(3):
        z[row + c, s * COLS : (s + 1) * COLS] = both[c * COLS : (c + 1) * COLS]


INNER, OUTER = ((0, 1), (1, 1), (0, 0), (1, 2)), ((0, 2), (1, 0))


def taps(z, which, w_space):
    sums = [0.0, 0.0]
    for i, (p, a) in enumerate(which):
        for c in range(3):
            sums[p] = sums[p] + dot(z[3 * i + c], w_space[3 * a + c])
    return sums


def inner_kernel(cot_in, video_in, w_time_in, w_space_in, cot, video, w_time, w_space, inner, grad, hidden, sems):
    copies = [
        pltpu.make_async_copy(source, target, sems.at[i])
        for i, (source, target) in enumerate(
            ((cot_in, cot), (w_space_in, w_space), (video_in, video), (w_time_in, w_time))
        )
    ]
    for copy in copies:
        copy.start()
    pick = picker()
    copies[0].wait()
    for s in range(2 * FRAMES):
        reach = [dot(pick, cot[s, p]) for p in range(2 * BAND)]
        for i, (p, a) in enumerate(INNER):
            put(inner, 3 * i, s, (reach[2 * p + 1 - a] + reach[2 * p + 2 - a]).astype(BF16))
    copies[1].wait()
    grad[...] = jnp.concatenate(taps(inner, INNER, w_space))
    copies[2].wait()
    copies[3].wait()
    hidden[:CELLS] = dot(video[:CELLS], w_time[2])
    hidden[CELLS:] = dot(video[:CELLS], w_time[1]) + dot(video[CELLS:], w_time[2])


def inner_terms(cot, video, w_time, w_space):
    cells = FRAMES * CELLS
    return pl.pallas_call(
        inner_kernel,
        name="inner_terms",
        out_shape=(
            *(jax.ShapeDtypeStruct(array.shape, BF16) for array in (cot, video, w_time, w_space)),
            jax.ShapeDtypeStruct((3 * len(INNER), HALF, CH_OUT), BF16),
            jax.ShapeDtypeStruct((2 * cells, CH_IN), F32),
            jax.ShapeDtypeStruct((cells, 2 * CH_IN), F32),
        ),
        in_specs=[pl.BlockSpec(memory_space=pltpu.HBM)] * 4,
        out_specs=(VMEM,) * 7,
        scratch_shapes=[pltpu.SemaphoreType.DMA((4,))],
        compiler_params=params(16),
        cost_estimate=pl.CostEstimate(flops=1_500_000_000, bytes_accessed=6_000_000, transcendentals=0),
    )(cot, video, w_time, w_space)


def grad_kernel(cot, low, high, w_space, grad_in, grad_hidden, outer):
    pick = picker()
    for s in range(2 * FRAMES):
        put(outer, 0, s, (dot(pick, low[s, 0]) + dot(pick, cot[s, 0])).astype(BF16))
        put(outer, 3, s, (dot(pick, cot[s, 2 * BAND - 1]) + dot(pick, high[s, 0])).astype(BF16))
    for p, part in enumerate(taps(outer, OUTER, w_space)):
        part = part + grad_in[p * HALF : (p + 1) * HALF]
        for t in range(FRAMES):
            for j in range(2):
                s = 2 * t + j
                grad_hidden[(t * BAND + p) * COLS : (t * BAND + p + 1) * COLS, j * CH_IN : (j + 1) * CH_IN] = part[
                    s * COLS : (s + 1) * COLS
                ].astype(BF16)


def grad_terms(cot, low, high, w_space, grad):
    return pl.pallas_call(
        grad_kernel,
        name="grad_terms",
        out_shape=(
            jax.ShapeDtypeStruct((FRAMES * CELLS, 2 * CH_IN), BF16),
            jax.ShapeDtypeStruct((3 * len(OUTER), HALF, CH_OUT), BF16),
        ),
        in_specs=[VMEM] * 5,
        out_specs=(VMEM,) * 2,
        compiler_params=params(8),
        cost_estimate=pl.CostEstimate(flops=800_000_000, bytes_accessed=4_000_000, transcendentals=0),
    )(cot, low, high, w_space, grad)


def block_kernel(
    video, carried, w_time, inner, outer, grad_hidden, hidden_in,
    keep, send,
    ext, hid, time_acc, space_acc,
):
    ext[0 : FRAMES * CELLS] = carried[...]
    ext[FRAMES * CELLS :] = video[...]
    first = hidden_in[:CELLS] + dot(carried[:CELLS], w_time[0]) + dot(carried[CELLS:], w_time[1])
    second = hidden_in[CELLS:] + dot(carried[CELLS:], w_time[0])
    for t, hidden in enumerate((first, second)):
        for p in range(BAND):
            for j in range(2):
                start = (p * 2 * FRAMES + 2 * t + j) * COLS
                hid[start : start + COLS] = hidden[
                    p * COLS : (p + 1) * COLS, j * CH_IN : (j + 1) * CH_IN
                ].astype(BF16)

    for k in range(3):
        time_acc[k * CH_IN : (k + 1) * CH_IN] = dot_t(ext[k * CELLS : (k + FRAMES) * CELLS], grad_hidden[...])
    hid_t = [hid[p * HALF : (p + 1) * HALF].T for p in range(BAND)]
    where = {key: (z, 3 * i) for z, order in ((inner, INNER), (outer, OUTER)) for i, key in enumerate(order)}
    for a in range(3):
        for c in range(3):
            total = 0.0
            for p in range(BAND):
                z, row = where[p, a]
                total = total + dot(hid_t[p], z[row + c])
            tap = 3 * a + c
            space_acc[tap * CH_IN : (tap + 1) * CH_IN] = total

    mine = lax.axis_index("clip") == 0
    half = SPACE_ROWS // 2
    for r in range(N_X * N_Z):
        xh, xl, zh, zl = r // N_Z // 2, r // N_Z % 2, r % N_Z // 2, r % 2
        t0, s0 = r * TIME_ROWS, r * SPACE_ROWS
        lines = [time_acc[t0 : t0 + TIME_ROWS, j * LANES : (j + 1) * LANES] for j in range(6)]
        lines.append(space_acc[s0 : s0 + SPACE_ROWS, 0:LANES])
        rest = [space_acc[s0 + i * half : s0 + (i + 1) * half, LANES:CH_OUT] for i in range(2)]
        lines.append(jnp.concatenate(rest, axis=1))
        lines.append(jnp.zeros((6, LANES), F32))
        lines = jnp.concatenate(lines, axis=0).astype(BF16)
        upper, lower = lines[: LINES // 2], lines[LINES // 2 :]
        mine_half, other_half = jnp.where(mine, upper, lower), jnp.where(mine, lower, upper)
        for c0 in range(2):
            for c1 in range(2):
                piece = (c0 * 2 + c1) * PIECE
                keep[xl, zl, c0, xh, c1, zh] = mine_half[piece : piece + PIECE]
                send[xl, zl, c0, xh, c1, zh] = other_half[piece : piece + PIECE]


def block_terms(video, carried, w_time, inner, outer, grad_hidden, hidden):
    cells = FRAMES * CELLS
    half = jax.ShapeDtypeStruct((2, 2, 2, N_X // 2, 2, N_Z // 2, PIECE, LANES), BF16)
    return pl.pallas_call(
        block_kernel,
        name="block_terms",
        out_shape=(half, half),
        in_specs=[VMEM] * 7,
        out_specs=(VMEM,) * 2,
        scratch_shapes=[
            pltpu.VMEM((2 * cells, CH_IN), BF16),
            pltpu.VMEM((2 * cells, CH_IN), BF16),
            pltpu.VMEM((3 * CH_IN, 2 * CH_IN), F32),
            pltpu.VMEM((9 * CH_IN, CH_OUT), F32),
        ],
        compiler_params=params(20),
        cost_estimate=pl.CostEstimate(flops=3_000_000_000, bytes_accessed=12_000_000, transcendentals=0),
    )(video, carried, w_time, inner, outer, grad_hidden, hidden)


def pair_kernel(a, b, out):
    out[...] = (a[...].astype(F32) + b[...].astype(F32)).astype(BF16)


def pair_sum(a, b):
    return pl.pallas_call(
        pair_kernel,
        name="pair_sum",
        out_shape=jax.ShapeDtypeStruct(a.shape, BF16),
        in_specs=[VMEM] * 2,
        out_specs=VMEM,
        compiler_params=params(8),
    )(a, b)


def group_kernel(copies, parts, out):
    total = parts[0].astype(F32)
    for i in range(1, parts.shape[0]):
        total = total + parts[i].astype(F32)
    total = total.astype(BF16)
    if copies is None:
        out[...] = total
    else:
        for i in range(copies):
            out[i] = total


def group_sum(parts, copies=None):
    lead = () if copies is None else (copies,)
    return pl.pallas_call(
        lambda *refs: group_kernel(copies, *refs),
        name="group_sum",
        out_shape=jax.ShapeDtypeStruct(lead + parts.shape[1:], BF16),
        in_specs=[VMEM],
        out_specs=VMEM,
        compiler_params=params(8),
    )(parts)


def unpack_kernel(scale, pieces, own, following, time, space, video, line):
    video[...] = (own[...] + following[...].astype(F32)).astype(BF16)
    for k in range(2):
        for c0 in range(2):
            for c1 in range(2):
                low = (c1 * 2 + c0) * 2 + k
                start = ((k * 2 + c0) * 2 + c1) * PIECE
                total = pieces[low].astype(F32) + pieces[8 + low].astype(F32)
                line[start : start + PIECE] = total * scale
    for j in range(6):
        time[:, j * LANES : (j + 1) * LANES] = line[j * TIME_ROWS : (j + 1) * TIME_ROWS].astype(BF16)
    space[0:LANES] = line[216 : 216 + LANES].T[:, :SPACE_ROWS].astype(BF16)
    half = SPACE_ROWS // 2
    rest = line[324 : 324 + 64].T
    space[LANES:] = jnp.concatenate([rest[0:64, :half], rest[64:, :half]], axis=1).astype(BF16)


def unpack(pieces, own, following, scale):
    return pl.pallas_call(
        lambda *refs: unpack_kernel(scale, *refs),
        name="unpack",
        out_shape=(
            jax.ShapeDtypeStruct((TIME_ROWS, 6 * LANES), BF16),
            jax.ShapeDtypeStruct((CH_OUT, SPACE_ROWS), BF16),
            jax.ShapeDtypeStruct(own.shape, BF16),
        ),
        in_specs=[VMEM] * 3,
        out_specs=(VMEM,) * 3,
        scratch_shapes=[pltpu.VMEM((LINES + 8, LANES), F32)],
        compiler_params=params(8),
    )(pieces, own, following)


def video_kernel(grad_hidden, w_time, ours, returned):
    first, second = grad_hidden[:CELLS], grad_hidden[CELLS:]
    ours[:CELLS] = dot_rows(first, w_time[2]) + dot_rows(second, w_time[1])
    ours[CELLS:] = dot_rows(second, w_time[2])
    returned[:CELLS] = dot_rows(first, w_time[0]).astype(BF16)
    returned[CELLS:] = (dot_rows(first, w_time[1]) + dot_rows(second, w_time[0])).astype(BF16)


def video_terms(grad_hidden, w_time):
    return pl.pallas_call(
        video_kernel,
        name="video_terms",
        out_shape=(
            jax.ShapeDtypeStruct((FRAMES * CELLS, CH_IN), F32),
            jax.ShapeDtypeStruct((FRAMES * CELLS, CH_IN), BF16),
        ),
        in_specs=[VMEM] * 2,
        out_specs=(VMEM,) * 2,
        compiler_params=params(8),
        cost_estimate=pl.CostEstimate(flops=700_000_000, bytes_accessed=2_500_000, transcendentals=0),
    )(grad_hidden, w_time)


def along(axis, steps):
    count = lax.axis_size(axis)
    return [(i, i + steps) for i in range(count) if 0 <= i + steps < count]


def exchange(parts, axes, groups=None):
    return lax.all_to_all(parts, axes, 0, 0, tiled=True, axis_index_groups=groups)


def local(video, cotangent, w_time, w_space):
    cot = cotangent[0]
    own = video[0].reshape(FRAMES * CELLS, CH_IN)
    rows, chain = lax.axis_size("rows"), lax.axis_size("chain")
    w_space = w_space.transpose(0, 1, 3, 2).reshape(9, CH_OUT, CH_IN)
    low = lax.ppermute(cot[:, 2 * BAND - 1 :], "rows", along("rows", 1))
    high = lax.ppermute(cot[:, :1], "rows", along("rows", -1))
    carried = lax.ppermute(own, "chain", along("chain", 1))
    operands = [pltpu.with_memory_space_constraint(value, pltpu.HBM) for value in (cot, own, w_time, w_space)]
    cot, own, w_time, w_space, inner, grad, hidden = inner_terms(*operands)
    grad_hidden, outer = grad_terms(cot, low, high, w_space, grad)
    keep, send = block_terms(own, carried, w_time, inner, outer, grad_hidden, hidden)
    received = lax.ppermute(send, "clip", [(0, 1), (1, 0)])
    ours, returned = video_terms(grad_hidden, w_time)
    received, ours = lax.optimization_barrier((received, ours))

    def device(c, x, z):
        return c * rows + x * N_Z + z

    def pair(index, core, count):
        return sorted(((2 * index + core) % count, (2 * index + core + 1) % count), key=lambda i: i % 2)

    near = [
        [
            2 * device(c, x, z) + core
            for x in pair(xh, core, N_X)
            for z in pair(zh, core, N_Z)
            for c in pair(ch, core, chain)
        ]
        for core in range(2)
        for xh in range(N_X // 2)
        for ch in range(chain // 2)
        for zh in range(N_Z // 2)
    ]
    far = [
        [
            device(4 * c2 + 2 * c + c0, 2 * xh + xl, 2 * zh + zl)
            for xh in range(N_X // 2)
            for c in range(2)
            for zh in range(N_Z // 2)
        ]
        for c2 in range(chain // 4)
        for c0 in range(2)
        for xl in range(2)
        for zl in range(2)
    ]
    share = pair_sum(keep.reshape(-1, LANES), received.reshape(-1, LANES))
    share, returned = lax.optimization_barrier((share, returned))
    following = lax.ppermute(returned, "chain", along("chain", -1))
    share = exchange(share.reshape(8, -1, LANES), ("chain", "rows", "clip"), near)
    share, following = lax.optimization_barrier((share, following))
    share = group_sum(exchange(group_sum(share).reshape(2 * N_Z, PIECE, LANES), ("chain", "rows"), far), 2 * chain)
    pieces = exchange(share, ("chain", "clip"))
    voxels = 2 * chain * 2 * FRAMES * rows * 2 * BAND * 2 * COLS
    grad_time, grad_space, grad_video = unpack(pieces, ours, following, 1.0 / math.sqrt(voxels))
    return grad_video.reshape(video.shape), grad_time, grad_space.T


def solution(mesh):
    placed = P("clip", "chain", "rows", None, None)
    return jax.shard_map(
        local,
        mesh=mesh,
        in_specs=(placed, placed, P(), P()),
        out_specs=(placed, P("rows", None), P("rows", None)),
        check_vma=False,
    )
```

```python
import math

import jax
import jax.numpy as jnp
from jax import lax
from jax.experimental import pallas as pl
from jax.experimental.pallas import tpu as pltpu
from jax.sharding import PartitionSpec as P

FRAMES, BAND, COLS, CH_IN, CH_OUT = 2, 2, 48, 384, 192
CELLS = BAND * COLS
N_X, N_Z = 4, 8
F32, BF16 = jnp.float32, jnp.bfloat16
LANES = 128
PIECE, LINES = 48, 384
TIME_ROWS, SPACE_ROWS = 36, 108
SPLIT = 12


def dot(a, b):
    return jnp.dot(a, b, preferred_element_type=F32)


def dot_rows(a, b):
    return lax.dot_general(a, b, (((1,), (1,)), ((), ())), preferred_element_type=F32)


def dot_t(a, b):
    return lax.dot_general(a, b, (((0,), (0,)), ((), ())), preferred_element_type=F32)


VMEM = pl.BlockSpec(memory_space=pltpu.VMEM)


def params(mib):
    return pltpu.CompilerParams(vmem_limit_bytes=mib * 1024 * 1024)


def picker():
    row = lax.broadcasted_iota(jnp.int32, (3 * COLS, 2 * COLS), 0)
    col = lax.broadcasted_iota(jnp.int32, (3 * COLS, 2 * COLS), 1)
    first = 2 * (row % COLS) + 1 - row // COLS
    return jnp.where((col == first) | (col == first + 1), 1.0, 0.0).astype(BF16)


HALF = 2 * FRAMES * COLS


def put(z, row, s, both):
    for c in range(3):
        z[row + c, s * COLS : (s + 1) * COLS] = both[c * COLS : (c + 1) * COLS]


INNER, OUTER = ((0, 1), (1, 1), (0, 0), (1, 2)), ((0, 2), (1, 0))


def taps(z, which, w_space):
    sums = [0.0, 0.0]
    for i, (p, a) in enumerate(which):
        for c in range(3):
            sums[p] = sums[p] + dot(z[3 * i + c], w_space[3 * a + c])
    return sums


def inner_kernel(cot_in, video_in, w_time_in, w_space_in, cot, video, w_time, w_space, inner, grad, hidden, sems):
    copies = [
        pltpu.make_async_copy(source, target, sems.at[i])
        for i, (source, target) in enumerate(
            ((cot_in, cot), (w_space_in, w_space), (video_in, video), (w_time_in, w_time))
        )
    ]
    for copy in copies:
        copy.start()
    pick = picker()
    copies[0].wait()
    for s in range(2 * FRAMES):
        reach = [dot(pick, cot[s, p]) for p in range(2 * BAND)]
        for i, (p, a) in enumerate(INNER):
            put(inner, 3 * i, s, (reach[2 * p + 1 - a] + reach[2 * p + 2 - a]).astype(BF16))
    copies[1].wait()
    grad[...] = jnp.concatenate(taps(inner, INNER, w_space))
    copies[2].wait()
    copies[3].wait()
    hidden[:CELLS] = dot(video[:CELLS], w_time[2])
    hidden[CELLS:] = dot(video[:CELLS], w_time[1]) + dot(video[CELLS:], w_time[2])


def inner_terms(cot, video, w_time, w_space):
    cells = FRAMES * CELLS
    return pl.pallas_call(
        inner_kernel,
        name="inner_terms",
        out_shape=(
            *(jax.ShapeDtypeStruct(array.shape, BF16) for array in (cot, video, w_time, w_space)),
            jax.ShapeDtypeStruct((3 * len(INNER), HALF, CH_OUT), BF16),
            jax.ShapeDtypeStruct((2 * cells, CH_IN), F32),
            jax.ShapeDtypeStruct((cells, 2 * CH_IN), F32),
        ),
        in_specs=[pl.BlockSpec(memory_space=pltpu.HBM)] * 4,
        out_specs=(VMEM,) * 7,
        scratch_shapes=[pltpu.SemaphoreType.DMA((4,))],
        compiler_params=params(16),
        cost_estimate=pl.CostEstimate(flops=1_500_000_000, bytes_accessed=6_000_000, transcendentals=0),
    )(cot, video, w_time, w_space)


def grad_kernel(cot, low, high, w_space, grad_in, grad_hidden, outer):
    pick = picker()
    for s in range(2 * FRAMES):
        put(outer, 0, s, (dot(pick, low[s, 0]) + dot(pick, cot[s, 0])).astype(BF16))
        put(outer, 3, s, (dot(pick, cot[s, 2 * BAND - 1]) + dot(pick, high[s, 0])).astype(BF16))
    for p, part in enumerate(taps(outer, OUTER, w_space)):
        part = part + grad_in[p * HALF : (p + 1) * HALF]
        for t in range(FRAMES):
            for j in range(2):
                s = 2 * t + j
                grad_hidden[(t * BAND + p) * COLS : (t * BAND + p + 1) * COLS, j * CH_IN : (j + 1) * CH_IN] = part[
                    s * COLS : (s + 1) * COLS
                ].astype(BF16)


def grad_terms(cot, low, high, w_space, grad):
    return pl.pallas_call(
        grad_kernel,
        name="grad_terms",
        out_shape=(
            jax.ShapeDtypeStruct((FRAMES * CELLS, 2 * CH_IN), BF16),
            jax.ShapeDtypeStruct((3 * len(OUTER), HALF, CH_OUT), BF16),
        ),
        in_specs=[VMEM] * 5,
        out_specs=(VMEM,) * 2,
        compiler_params=params(8),
        cost_estimate=pl.CostEstimate(flops=800_000_000, bytes_accessed=4_000_000, transcendentals=0),
    )(cot, low, high, w_space, grad)


def time_half(ext, grad_hidden, out, time_acc):
    for k in range(3):
        time_acc[k * CH_IN : (k + 1) * CH_IN] = dot_t(ext[k * CELLS : (k + FRAMES) * CELLS], grad_hidden[...])
    for r in range(N_X * N_Z):
        t0 = r * TIME_ROWS
        lines = [time_acc[t0 : t0 + TIME_ROWS, j * LANES : (j + 1) * LANES] for j in range(5)]
        lines.append(time_acc[t0 : t0 + SPLIT, 5 * LANES :])
        put_lines(out, r, lines)


def space_half(ext, carried, w_time, inner, outer, grad_hidden, hidden_in, out, hid, time_acc, space_acc):
    first = hidden_in[:CELLS] + dot(carried[:CELLS], w_time[0]) + dot(carried[CELLS:], w_time[1])
    second = hidden_in[CELLS:] + dot(carried[CELLS:], w_time[0])
    for t, hidden in enumerate((first, second)):
        for p in range(BAND):
            for j in range(2):
                start = (p * 2 * FRAMES + 2 * t + j) * COLS
                hid[start : start + COLS] = hidden[
                    p * COLS : (p + 1) * COLS, j * CH_IN : (j + 1) * CH_IN
                ].astype(BF16)
    for k in range(3):
        time_acc[k * CH_IN : (k + 1) * CH_IN, 5 * LANES :] = dot_t(
            ext[k * CELLS : (k + FRAMES) * CELLS], grad_hidden[:, 5 * LANES :]
        )
    hid_t = [hid[p * HALF : (p + 1) * HALF].T for p in range(BAND)]
    where = {key: (z, 3 * i) for z, order in ((inner, INNER), (outer, OUTER)) for i, key in enumerate(order)}
    for a in range(3):
        for c in range(3):
            total = 0.0
            for p in range(BAND):
                z, row = where[p, a]
                total = total + dot(hid_t[p], z[row + c])
            tap = 3 * a + c
            space_acc[tap * CH_IN : (tap + 1) * CH_IN] = total
    half = SPACE_ROWS // 2
    for r in range(N_X * N_Z):
        t0, s0 = r * TIME_ROWS, r * SPACE_ROWS
        rest = [space_acc[s0 + i * half : s0 + (i + 1) * half, LANES:CH_OUT] for i in range(2)]
        lines = [
            time_acc[t0 + SPLIT : t0 + TIME_ROWS, 5 * LANES :],
            space_acc[s0 : s0 + SPACE_ROWS, 0:LANES],
            jnp.concatenate(rest, axis=1),
            jnp.zeros((6, LANES), F32),
        ]
        put_lines(out, r, lines)


def put_lines(out, r, lines):
    xh, xl, zh, zl = r // N_Z // 2, r // N_Z % 2, r % N_Z // 2, r % 2
    lines = jnp.concatenate(lines, axis=0).astype(BF16)
    for c0 in range(2):
        for c1 in range(2):
            piece = (c0 * 2 + c1) * PIECE
            out[xl, zl, c0, xh, c1, zh] = lines[piece : piece + PIECE]


def half_kernel(
    flip, video, carried, w_time, inner, outer, grad_hidden, hidden_in, out, ext, hid, time_acc, space_acc
):
    ext[0 : FRAMES * CELLS] = carried[...]
    ext[FRAMES * CELLS :] = video[...]
    first = lax.axis_index("clip") == flip

    @pl.when(first)
    def _():
        time_half(ext, grad_hidden, out, time_acc)

    @pl.when(jnp.logical_not(first))
    def _():
        space_half(ext, carried, w_time, inner, outer, grad_hidden, hidden_in, out, hid, time_acc, space_acc)


def half_terms(flip, video, carried, w_time, inner, outer, grad_hidden, hidden):
    cells = FRAMES * CELLS
    return pl.pallas_call(
        lambda *refs: half_kernel(flip, *refs),
        name="send_terms" if flip else "keep_terms",
        out_shape=jax.ShapeDtypeStruct((2, 2, 2, N_X // 2, 2, N_Z // 2, PIECE, LANES), BF16),
        in_specs=[VMEM] * 7,
        out_specs=VMEM,
        scratch_shapes=[
            pltpu.VMEM((2 * cells, CH_IN), BF16),
            pltpu.VMEM((2 * cells, CH_IN), BF16),
            pltpu.VMEM((3 * CH_IN, 2 * CH_IN), F32),
            pltpu.VMEM((9 * CH_IN, CH_OUT), F32),
        ],
        compiler_params=params(20),
        cost_estimate=pl.CostEstimate(flops=1_500_000_000, bytes_accessed=6_000_000, transcendentals=0),
    )(video, carried, w_time, inner, outer, grad_hidden, hidden)


def pair_kernel(a, b, out):
    out[...] = (a[...].astype(F32) + b[...].astype(F32)).astype(BF16)


def pair_sum(a, b):
    return pl.pallas_call(
        pair_kernel,
        name="pair_sum",
        out_shape=jax.ShapeDtypeStruct(a.shape, BF16),
        in_specs=[VMEM] * 2,
        out_specs=VMEM,
        compiler_params=params(8),
    )(a, b)


def group_kernel(copies, parts, out):
    total = parts[0].astype(F32)
    for i in range(1, parts.shape[0]):
        total = total + parts[i].astype(F32)
    total = total.astype(BF16)
    if copies is None:
        out[...] = total
    else:
        for i in range(copies):
            out[i] = total


def group_sum(parts, copies=None):
    lead = () if copies is None else (copies,)
    return pl.pallas_call(
        lambda *refs: group_kernel(copies, *refs),
        name="group_sum",
        out_shape=jax.ShapeDtypeStruct(lead + parts.shape[1:], BF16),
        in_specs=[VMEM],
        out_specs=VMEM,
        compiler_params=params(8),
    )(parts)


def unpack_kernel(scale, pieces, own, following, time, space, video, line):
    video[...] = (own[...] + following[...].astype(F32)).astype(BF16)
    for k in range(2):
        for c0 in range(2):
            for c1 in range(2):
                low = (c1 * 2 + c0) * 2 + k
                start = ((k * 2 + c0) * 2 + c1) * PIECE
                total = pieces[low].astype(F32) + pieces[8 + low].astype(F32)
                line[start : start + PIECE] = total * scale
    for j in range(6):
        time[:, j * LANES : (j + 1) * LANES] = line[j * TIME_ROWS : (j + 1) * TIME_ROWS].astype(BF16)
    space[0:LANES] = line[216 : 216 + LANES].T[:, :SPACE_ROWS].astype(BF16)
    half = SPACE_ROWS // 2
    rest = line[324 : 324 + 64].T
    space[LANES:] = jnp.concatenate([rest[0:64, :half], rest[64:, :half]], axis=1).astype(BF16)


def unpack(pieces, own, following, scale):
    return pl.pallas_call(
        lambda *refs: unpack_kernel(scale, *refs),
        name="unpack",
        out_shape=(
            jax.ShapeDtypeStruct((TIME_ROWS, 6 * LANES), BF16),
            jax.ShapeDtypeStruct((CH_OUT, SPACE_ROWS), BF16),
            jax.ShapeDtypeStruct(own.shape, BF16),
        ),
        in_specs=[VMEM] * 3,
        out_specs=(VMEM,) * 3,
        scratch_shapes=[pltpu.VMEM((LINES + 8, LANES), F32)],
        compiler_params=params(8),
    )(pieces, own, following)


def video_kernel(grad_hidden, w_time, ours, returned):
    first, second = grad_hidden[:CELLS], grad_hidden[CELLS:]
    ours[:CELLS] = dot_rows(first, w_time[2]) + dot_rows(second, w_time[1])
    ours[CELLS:] = dot_rows(second, w_time[2])
    returned[:CELLS] = dot_rows(first, w_time[0]).astype(BF16)
    returned[CELLS:] = (dot_rows(first, w_time[1]) + dot_rows(second, w_time[0])).astype(BF16)


def video_terms(grad_hidden, w_time):
    return pl.pallas_call(
        video_kernel,
        name="video_terms",
        out_shape=(
            jax.ShapeDtypeStruct((FRAMES * CELLS, CH_IN), F32),
            jax.ShapeDtypeStruct((FRAMES * CELLS, CH_IN), BF16),
        ),
        in_specs=[VMEM] * 2,
        out_specs=(VMEM,) * 2,
        compiler_params=params(8),
        cost_estimate=pl.CostEstimate(flops=700_000_000, bytes_accessed=2_500_000, transcendentals=0),
    )(grad_hidden, w_time)


def along(axis, steps):
    count = lax.axis_size(axis)
    return [(i, i + steps) for i in range(count) if 0 <= i + steps < count]


def exchange(parts, axes, groups=None):
    return lax.all_to_all(parts, axes, 0, 0, tiled=True, axis_index_groups=groups)


def local(video, cotangent, w_time, w_space):
    cot = cotangent[0]
    own = video[0].reshape(FRAMES * CELLS, CH_IN)
    rows, chain = lax.axis_size("rows"), lax.axis_size("chain")
    w_space = w_space.transpose(0, 1, 3, 2).reshape(9, CH_OUT, CH_IN)
    low = lax.ppermute(cot[:, 2 * BAND - 1 :], "rows", along("rows", 1))
    high = lax.ppermute(cot[:, :1], "rows", along("rows", -1))
    carried = lax.ppermute(own, "chain", along("chain", 1))
    operands = [pltpu.with_memory_space_constraint(value, pltpu.HBM) for value in (cot, own, w_time, w_space)]
    cot, own, w_time, w_space, inner, grad, hidden = inner_terms(*operands)
    grad_hidden, outer = grad_terms(cot, low, high, w_space, grad)
    terms = (own, carried, w_time, inner, outer, grad_hidden, hidden)
    send = half_terms(1, *terms)
    received = lax.ppermute(send, "clip", [(0, 1), (1, 0)])
    keep = half_terms(0, *terms)
    ours, returned = video_terms(grad_hidden, w_time)
    received, ours, keep = lax.optimization_barrier((received, ours, keep))

    def device(c, x, z):
        return c * rows + x * N_Z + z

    def pair(index, core, count):
        return sorted(((2 * index + core) % count, (2 * index + core + 1) % count), key=lambda i: i % 2)

    near = [
        [
            2 * device(c, x, z) + core
            for x in pair(xh, core, N_X)
            for z in pair(zh, core, N_Z)
            for c in pair(ch, core, chain)
        ]
        for core in range(2)
        for xh in range(N_X // 2)
        for ch in range(chain // 2)
        for zh in range(N_Z // 2)
    ]
    far = [
        [
            device(4 * c2 + 2 * c + c0, 2 * xh + xl, 2 * zh + zl)
            for xh in range(N_X // 2)
            for c in range(2)
            for zh in range(N_Z // 2)
        ]
        for c2 in range(chain // 4)
        for c0 in range(2)
        for xl in range(2)
        for zl in range(2)
    ]
    share = pair_sum(keep.reshape(-1, LANES), received.reshape(-1, LANES))
    share = group_sum(exchange(share.reshape(8, -1, LANES), ("chain", "rows", "clip"), near))
    share, returned = lax.optimization_barrier((share, returned))
    following = lax.ppermute(returned, "chain", along("chain", -1))
    share, following = lax.optimization_barrier((exchange(share.reshape(2 * N_Z, PIECE, LANES), ("chain", "rows"), far), following))
    share = group_sum(share, 2 * chain)
    pieces = exchange(share, ("chain", "clip"))
    voxels = 2 * chain * 2 * FRAMES * rows * 2 * BAND * 2 * COLS
    grad_time, grad_space, grad_video = unpack(pieces, ours, following, 1.0 / math.sqrt(voxels))
    return grad_video.reshape(video.shape), grad_time, grad_space.T


def solution(mesh):
    placed = P("clip", "chain", "rows", None, None)
    return jax.shard_map(
        local,
        mesh=mesh,
        in_specs=(placed, placed, P(), P()),
        out_specs=(placed, P("rows", None), P("rows", None)),
        check_vma=False,
    )
```

```python
import math

import jax
import jax.numpy as jnp
from jax import lax
from jax.experimental import pallas as pl
from jax.experimental.pallas import tpu as pltpu
from jax.sharding import PartitionSpec as P

FRAMES, BAND, COLS, CH_IN, CH_OUT = 2, 2, 48, 384, 192
CELLS = BAND * COLS
N_X, N_Z = 4, 8
F32, BF16 = jnp.float32, jnp.bfloat16
LANES = 128
PIECE, LINES = 48, 384
TIME_ROWS, SPACE_ROWS = 36, 108


def dot(a, b):
    return jnp.dot(a, b, preferred_element_type=F32)


def dot_rows(a, b):
    return lax.dot_general(a, b, (((1,), (1,)), ((), ())), preferred_element_type=F32)


def dot_t(a, b):
    return lax.dot_general(a, b, (((0,), (0,)), ((), ())), preferred_element_type=F32)


VMEM = pl.BlockSpec(memory_space=pltpu.VMEM)


def params(mib):
    return pltpu.CompilerParams(vmem_limit_bytes=mib * 1024 * 1024)


def picker():
    row = lax.broadcasted_iota(jnp.int32, (3 * COLS, 2 * COLS), 0)
    col = lax.broadcasted_iota(jnp.int32, (3 * COLS, 2 * COLS), 1)
    first = 2 * (row % COLS) + 1 - row // COLS
    return jnp.where((col == first) | (col == first + 1), 1.0, 0.0).astype(BF16)


HALF = 2 * FRAMES * COLS


def put(z, row, s, both):
    for c in range(3):
        z[row + c, s * COLS : (s + 1) * COLS] = both[c * COLS : (c + 1) * COLS]


INNER, OUTER = ((0, 1), (1, 1), (0, 0), (1, 2)), ((0, 2), (1, 0))


def taps(z, which, w_space):
    sums = [0.0, 0.0]
    for i, (p, a) in enumerate(which):
        for c in range(3):
            sums[p] = sums[p] + dot(z[3 * i + c], w_space[3 * a + c])
    return sums


def inner_kernel(cot_in, video_in, w_time_in, w_space_in, cot, video, w_time, w_space, inner, grad, hidden, sems):
    pieces = [(cot_in.at[s], cot.at[s]) for s in range(2 * FRAMES)]
    pieces += [(w_space_in.at[pl.ds(3 * a, 3)], w_space.at[pl.ds(3 * a, 3)]) for a in (1, 0, 2)]
    pieces += [(video_in, video), (w_time_in.at[pl.ds(1, 2)], w_time.at[pl.ds(1, 2)]), (w_time_in.at[0], w_time.at[0])]
    copies = [pltpu.make_async_copy(source, target, sems.at[i]) for i, (source, target) in enumerate(pieces)]
    for copy in copies:
        copy.start()
    pick = picker()
    for s in range(2 * FRAMES):
        copies[s].wait()
        reach = [dot(pick, cot[s, p]) for p in range(2 * BAND)]
        for i, (p, a) in enumerate(INNER):
            put(inner, 3 * i, s, (reach[2 * p + 1 - a] + reach[2 * p + 2 - a]).astype(BF16))
    sums = [0.0, 0.0]
    for i, (p, a) in enumerate(INNER):
        if i != 1:
            copies[2 * FRAMES + max(i - 1, 0)].wait()
        for c in range(3):
            sums[p] = sums[p] + dot(inner[3 * i + c], w_space[3 * a + c])
    grad[...] = jnp.concatenate(sums)
    for copy in copies[2 * FRAMES + 3 : -1]:
        copy.wait()
    hidden[:CELLS] = dot(video[:CELLS], w_time[2])
    hidden[CELLS:] = dot(video[:CELLS], w_time[1]) + dot(video[CELLS:], w_time[2])
    copies[-1].wait()


def inner_terms(cot, video, w_time, w_space):
    cells = FRAMES * CELLS
    return pl.pallas_call(
        inner_kernel,
        name="inner_terms",
        out_shape=(
            *(jax.ShapeDtypeStruct(array.shape, BF16) for array in (cot, video, w_time, w_space)),
            jax.ShapeDtypeStruct((3 * len(INNER), HALF, CH_OUT), BF16),
            jax.ShapeDtypeStruct((2 * cells, CH_IN), F32),
            jax.ShapeDtypeStruct((cells, 2 * CH_IN), F32),
        ),
        in_specs=[pl.BlockSpec(memory_space=pltpu.HBM)] * 4,
        out_specs=(VMEM,) * 7,
        scratch_shapes=[pltpu.SemaphoreType.DMA((2 * FRAMES + 6,))],
        compiler_params=params(16),
        cost_estimate=pl.CostEstimate(flops=1_500_000_000, bytes_accessed=6_000_000, transcendentals=0),
    )(cot, video, w_time, w_space)


def grad_kernel(cot, low, high, w_space, grad_in, grad_hidden, outer):
    pick = picker()
    for s in range(2 * FRAMES):
        put(outer, 0, s, (dot(pick, low[s, 0]) + dot(pick, cot[s, 0])).astype(BF16))
        put(outer, 3, s, (dot(pick, cot[s, 2 * BAND - 1]) + dot(pick, high[s, 0])).astype(BF16))
    for p, part in enumerate(taps(outer, OUTER, w_space)):
        part = part + grad_in[p * HALF : (p + 1) * HALF]
        for t in range(FRAMES):
            for j in range(2):
                s = 2 * t + j
                grad_hidden[(t * BAND + p) * COLS : (t * BAND + p + 1) * COLS, j * CH_IN : (j + 1) * CH_IN] = part[
                    s * COLS : (s + 1) * COLS
                ].astype(BF16)


def grad_terms(cot, low, high, w_space, grad):
    return pl.pallas_call(
        grad_kernel,
        name="grad_terms",
        out_shape=(
            jax.ShapeDtypeStruct((FRAMES * CELLS, 2 * CH_IN), BF16),
            jax.ShapeDtypeStruct((3 * len(OUTER), HALF, CH_OUT), BF16),
        ),
        in_specs=[VMEM] * 5,
        out_specs=(VMEM,) * 2,
        compiler_params=params(8),
        cost_estimate=pl.CostEstimate(flops=800_000_000, bytes_accessed=4_000_000, transcendentals=0),
    )(cot, low, high, w_space, grad)


def block_kernel(
    video, carried, w_time, inner, outer, grad_hidden, hidden_in,
    keep, send,
    ext, hid, time_acc, space_acc,
):
    ext[0 : FRAMES * CELLS] = carried[...]
    ext[FRAMES * CELLS :] = video[...]
    first = hidden_in[:CELLS] + dot(carried[:CELLS], w_time[0]) + dot(carried[CELLS:], w_time[1])
    second = hidden_in[CELLS:] + dot(carried[CELLS:], w_time[0])
    for t, hidden in enumerate((first, second)):
        for p in range(BAND):
            for j in range(2):
                start = (p * 2 * FRAMES + 2 * t + j) * COLS
                hid[start : start + COLS] = hidden[
                    p * COLS : (p + 1) * COLS, j * CH_IN : (j + 1) * CH_IN
                ].astype(BF16)

    for k in range(3):
        time_acc[k * CH_IN : (k + 1) * CH_IN] = dot_t(ext[k * CELLS : (k + FRAMES) * CELLS], grad_hidden[...])
    hid_t = [hid[p * HALF : (p + 1) * HALF].T for p in range(BAND)]
    where = {key: (z, 3 * i) for z, order in ((inner, INNER), (outer, OUTER)) for i, key in enumerate(order)}
    for a in range(3):
        for c in range(3):
            total = 0.0
            for p in range(BAND):
                z, row = where[p, a]
                total = total + dot(hid_t[p], z[row + c])
            tap = 3 * a + c
            space_acc[tap * CH_IN : (tap + 1) * CH_IN] = total

    mine = lax.axis_index("clip") == 0
    half = SPACE_ROWS // 2
    for r in range(N_X * N_Z):
        xh, xl, zh, zl = r // N_Z // 2, r // N_Z % 2, r % N_Z // 2, r % 2
        t0, s0 = r * TIME_ROWS, r * SPACE_ROWS
        lines = [time_acc[t0 : t0 + TIME_ROWS, j * LANES : (j + 1) * LANES] for j in range(6)]
        lines.append(space_acc[s0 : s0 + SPACE_ROWS, 0:LANES])
        rest = [space_acc[s0 + i * half : s0 + (i + 1) * half, LANES:CH_OUT] for i in range(2)]
        lines.append(jnp.concatenate(rest, axis=1))
        lines.append(jnp.zeros((6, LANES), F32))
        lines = jnp.concatenate(lines, axis=0).astype(BF16)
        upper, lower = lines[: LINES // 2], lines[LINES // 2 :]
        mine_half, other_half = jnp.where(mine, upper, lower), jnp.where(mine, lower, upper)
        for c0 in range(2):
            for c1 in range(2):
                piece = (c0 * 2 + c1) * PIECE
                keep[xl, zl, c0, xh, c1, zh] = mine_half[piece : piece + PIECE]
                send[xl, zl, c0, xh, c1, zh] = other_half[piece : piece + PIECE]


def block_terms(video, carried, w_time, inner, outer, grad_hidden, hidden):
    cells = FRAMES * CELLS
    half = jax.ShapeDtypeStruct((2, 2, 2, N_X // 2, 2, N_Z // 2, PIECE, LANES), BF16)
    return pl.pallas_call(
        block_kernel,
        name="block_terms",
        out_shape=(half, half),
        in_specs=[VMEM] * 7,
        out_specs=(VMEM,) * 2,
        scratch_shapes=[
            pltpu.VMEM((2 * cells, CH_IN), BF16),
            pltpu.VMEM((2 * cells, CH_IN), BF16),
            pltpu.VMEM((3 * CH_IN, 2 * CH_IN), F32),
            pltpu.VMEM((9 * CH_IN, CH_OUT), F32),
        ],
        compiler_params=params(20),
        cost_estimate=pl.CostEstimate(flops=3_000_000_000, bytes_accessed=12_000_000, transcendentals=0),
    )(video, carried, w_time, inner, outer, grad_hidden, hidden)


def pair_kernel(a, b, out):
    out[...] = (a[...].astype(F32) + b[...].astype(F32)).astype(BF16)


def pair_sum(a, b):
    return pl.pallas_call(
        pair_kernel,
        name="pair_sum",
        out_shape=jax.ShapeDtypeStruct(a.shape, BF16),
        in_specs=[VMEM] * 2,
        out_specs=VMEM,
        compiler_params=params(8),
    )(a, b)


def group_kernel(copies, parts, out):
    total = parts[0].astype(F32)
    for i in range(1, parts.shape[0]):
        total = total + parts[i].astype(F32)
    total = total.astype(BF16)
    if copies is None:
        out[...] = total
    else:
        for i in range(copies):
            out[i] = total


def group_sum(parts, copies=None):
    lead = () if copies is None else (copies,)
    return pl.pallas_call(
        lambda *refs: group_kernel(copies, *refs),
        name="group_sum",
        out_shape=jax.ShapeDtypeStruct(lead + parts.shape[1:], BF16),
        in_specs=[VMEM],
        out_specs=VMEM,
        compiler_params=params(8),
    )(parts)


def unpack_kernel(scale, pieces, own, following, time, space, video, line):
    video[...] = (own[...] + following[...].astype(F32)).astype(BF16)
    for k in range(2):
        for c0 in range(2):
            for c1 in range(2):
                low = (c1 * 2 + c0) * 2 + k
                start = ((k * 2 + c0) * 2 + c1) * PIECE
                total = pieces[low].astype(F32) + pieces[8 + low].astype(F32)
                line[start : start + PIECE] = total * scale
    for j in range(6):
        time[:, j * LANES : (j + 1) * LANES] = line[j * TIME_ROWS : (j + 1) * TIME_ROWS].astype(BF16)
    space[0:LANES] = line[216 : 216 + LANES].T[:, :SPACE_ROWS].astype(BF16)
    half = SPACE_ROWS // 2
    rest = line[324 : 324 + 64].T
    space[LANES:] = jnp.concatenate([rest[0:64, :half], rest[64:, :half]], axis=1).astype(BF16)


def unpack(pieces, own, following, scale):
    return pl.pallas_call(
        lambda *refs: unpack_kernel(scale, *refs),
        name="unpack",
        out_shape=(
            jax.ShapeDtypeStruct((TIME_ROWS, 6 * LANES), BF16),
            jax.ShapeDtypeStruct((CH_OUT, SPACE_ROWS), BF16),
            jax.ShapeDtypeStruct(own.shape, BF16),
        ),
        in_specs=[VMEM] * 3,
        out_specs=(VMEM,) * 3,
        scratch_shapes=[pltpu.VMEM((LINES + 8, LANES), F32)],
        compiler_params=params(8),
    )(pieces, own, following)


def video_kernel(grad_hidden, w_time, ours, returned):
    first, second = grad_hidden[:CELLS], grad_hidden[CELLS:]
    ours[:CELLS] = dot_rows(first, w_time[2]) + dot_rows(second, w_time[1])
    ours[CELLS:] = dot_rows(second, w_time[2])
    returned[:CELLS] = dot_rows(first, w_time[0]).astype(BF16)
    returned[CELLS:] = (dot_rows(first, w_time[1]) + dot_rows(second, w_time[0])).astype(BF16)


def video_terms(grad_hidden, w_time):
    return pl.pallas_call(
        video_kernel,
        name="video_terms",
        out_shape=(
            jax.ShapeDtypeStruct((FRAMES * CELLS, CH_IN), F32),
            jax.ShapeDtypeStruct((FRAMES * CELLS, CH_IN), BF16),
        ),
        in_specs=[VMEM] * 2,
        out_specs=(VMEM,) * 2,
        compiler_params=params(8),
        cost_estimate=pl.CostEstimate(flops=700_000_000, bytes_accessed=2_500_000, transcendentals=0),
    )(grad_hidden, w_time)


def along(axis, steps):
    count = lax.axis_size(axis)
    return [(i, i + steps) for i in range(count) if 0 <= i + steps < count]


def exchange(parts, axes, groups=None):
    return lax.all_to_all(parts, axes, 0, 0, tiled=True, axis_index_groups=groups)


def local(video, cotangent, w_time, w_space):
    cot = cotangent[0]
    own = video[0].reshape(FRAMES * CELLS, CH_IN)
    rows, chain = lax.axis_size("rows"), lax.axis_size("chain")
    w_space = w_space.transpose(0, 1, 3, 2).reshape(9, CH_OUT, CH_IN)
    low = lax.ppermute(cot[:, 2 * BAND - 1 :], "rows", along("rows", 1))
    high = lax.ppermute(cot[:, :1], "rows", along("rows", -1))
    carried = lax.ppermute(own, "chain", along("chain", 1))
    operands = [pltpu.with_memory_space_constraint(value, pltpu.HBM) for value in (cot, own, w_time, w_space)]
    cot, own, w_time, w_space, inner, grad, hidden = inner_terms(*operands)
    grad_hidden, outer = grad_terms(cot, low, high, w_space, grad)
    keep, send = block_terms(own, carried, w_time, inner, outer, grad_hidden, hidden)
    received = lax.ppermute(send, "clip", [(0, 1), (1, 0)])
    ours, returned = video_terms(grad_hidden, w_time)
    received, ours = lax.optimization_barrier((received, ours))

    def device(c, x, z):
        return c * rows + x * N_Z + z

    def pair(index, core, count):
        return sorted(((2 * index + core) % count, (2 * index + core + 1) % count), key=lambda i: i % 2)

    near = [
        [
            2 * device(c, x, z) + core
            for x in pair(xh, core, N_X)
            for z in pair(zh, core, N_Z)
            for c in pair(ch, core, chain)
        ]
        for core in range(2)
        for xh in range(N_X // 2)
        for ch in range(chain // 2)
        for zh in range(N_Z // 2)
    ]
    far = [
        [
            device(4 * c2 + 2 * c + c0, 2 * xh + xl, 2 * zh + zl)
            for xh in range(N_X // 2)
            for c in range(2)
            for zh in range(N_Z // 2)
        ]
        for c2 in range(chain // 4)
        for c0 in range(2)
        for xl in range(2)
        for zl in range(2)
    ]
    share = pair_sum(keep.reshape(-1, LANES), received.reshape(-1, LANES))
    share = group_sum(exchange(share.reshape(8, -1, LANES), ("chain", "rows", "clip"), near))
    share, returned = lax.optimization_barrier((share, returned))
    following = lax.ppermute(returned, "chain", along("chain", -1))
    share, following = lax.optimization_barrier((exchange(share.reshape(2 * N_Z, PIECE, LANES), ("chain", "rows"), far), following))
    share = group_sum(share, 2 * chain)
    pieces = exchange(share, ("chain", "clip"))
    voxels = 2 * chain * 2 * FRAMES * rows * 2 * BAND * 2 * COLS
    grad_time, grad_space, grad_video = unpack(pieces, ours, following, 1.0 / math.sqrt(voxels))
    return grad_video.reshape(video.shape), grad_time, grad_space.T


def solution(mesh):
    placed = P("clip", "chain", "rows", None, None)
    return jax.shard_map(
        local,
        mesh=mesh,
        in_specs=(placed, placed, P(), P()),
        out_specs=(placed, P("rows", None), P("rows", None)),
        check_vma=False,
    )
```
